32 devices in a mesh: slab: 4 (over y, x), point: 2 (over core), win: 4 (over z).
Axes of the slice: x: 2, y: 2, z: 4, core: 2. Of those that a mesh axis runs over, the one named last changes fastest.
Arguments:
- diag_blocks: float32 [4, 2, 256, 256], P('slab'), as said below
- couplings: float32 [4, 2, 256, 256], P('slab'), may hold values from -0.25 to 0.25
- subspace: float32 [8, 4, 2, 256, 128], P('win', 'slab'), may hold values from -6 to 6
- widths: int32 [8], P('win'), may hold values from 32 to 128, as said below
- owner_order: int32 [8], replicated, may hold values from 0 to 7, each once
- centers: float32 [8], P('win'), may hold values from -2.5 to 2.5
- radii: float32 [8], P('win'), may hold values from 0.6 to 1.5
Outputs:
- filtered: float32 [8, 4, 2, 256, 128], P('win', 'slab', None, 'point')
The draws below stay inside these ranges and needn't reach their ends.
Inputs may be any that keep to these rules, and one draw needn't show every extreme that they name: `widths`: columns in use of each window; some window uses all 128. `owner_order`: a permutation of the windows. `diag_blocks`: each diagonal block is Hermitian: index 0 symmetric, index 1 antisymmetric.
All inputs are finite; a program needn't handle non-finite values.
Results may differ from the reference program's by a relative error of at most 0.0003.
Values sent between devices are 32-bit elements; how exact they have to be, the bound alone decides.
No kernel may reach another device: no remote copies, remote signals or barrier semaphores. Data moves between devices by JAX's collectives and lax.ppermute only.
A program may use at most 128 MiB of HBM per device.

```python
import math
import jax
import jax.numpy as jnp
from jax import lax

B = 256
MCOL = 128
LAYERS = 4
WINDOWS = 8
N_POINT = 2


def draw_diag_blocks(key, part):
    first, second, third = jax.random.split(jax.random.fold_in(key, 11), 3)
    real_raw = jax.random.normal(first, (LAYERS, B, B), jnp.float32)
    imag_raw = jax.random.normal(second, (LAYERS, B, B), jnp.float32)
    scale_factor = B ** (-0.5)
    real_sym = 0.5 * (real_raw + jnp.swapaxes(real_raw, 1, 2)) * scale_factor
    imag_anti = 0.5 * (imag_raw - jnp.swapaxes(imag_raw, 1, 2)) * scale_factor
    onsite = jax.random.uniform(third, (LAYERS, B), jnp.float32, -1.5, 1.5)
    real_sym = real_sym + onsite[:, :, None] * jnp.eye(B, dtype=jnp.float32)[None]
    return jnp.stack([real_sym, imag_anti], axis=1).astype(jnp.float32)


def draw_widths(key, part):
    first, second = jax.random.split(jax.random.fold_in(key, 23))
    counts = jax.random.randint(first, (WINDOWS,), MCOL // 4, MCOL + 1)
    fullest = jax.random.randint(second, (), 0, WINDOWS)
    return jnp.where(jnp.arange(WINDOWS, dtype=jnp.int32) == fullest, MCOL, counts).astype(jnp.int32)


def level_of(key, shape, shards, smallest, largest):
    loudness = 1.0
    for position, blocks in shards:
        heights = jax.random.uniform(jax.random.fold_in(jax.random.fold_in(key, 6), position), (blocks,), jnp.float32, smallest / len(shards), largest / len(shards))
        loudness = loudness * jnp.repeat(jnp.exp(heights), shape[position] // blocks).reshape((-1,) + (1,) * (len(shape) - 1 - position))
    return loudness


def scatter_about(rng, dims, deviation, reach, cuts=(), kind=jnp.bfloat16):
    gain = level_of(rng, dims, cuts, -0.22, 0.18) if cuts else 1.0
    values = jax.random.normal(rng, dims, jnp.float32) * deviation * gain
    return jnp.minimum(jnp.maximum(values, -reach), reach).astype(kind)


def setup_inputs(seed: int = 0) -> dict:
    splits = jax.random.split(jax.random.key(seed), 8)
    diag_blocks = draw_diag_blocks(jax.random.fold_in(splits[7], 71), 0)
    couplings = scatter_about(splits[1], (LAYERS, 2, B, B), (2 * B) ** -0.5, 0.25, ((0, 4),), jnp.float32)
    subspace = scatter_about(splits[2], (WINDOWS, LAYERS, 2, B, MCOL), 1.0, 6.0, ((0, 4), (1, 4)), jnp.float32)
    widths = draw_widths(jax.random.fold_in(splits[7], 71), 0)
    owner_order = jax.random.permutation(splits[4], WINDOWS).astype(jnp.int32)
    centers = jnp.clip(jax.random.uniform(splits[5], (WINDOWS,), jnp.float32, -2.5, 2.5) * level_of(splits[5], (WINDOWS,), ((0, 4),), -0.4, 0.0), -2.5, 2.5)
    radii = jnp.clip(jnp.exp(math.log(1.5) - 0.9162907 * jax.random.uniform(splits[6], (WINDOWS,), jnp.float32) ** level_of(splits[6], (WINDOWS,), ((0, 4),), -0.2, 0.2)), 0.6, 1.5)
    return {"diag_blocks": diag_blocks, "couplings": couplings, "subspace": subspace, "widths": widths, "owner_order": owner_order, "centers": centers, "radii": radii}


HIGHEST_PRECISION = lax.Precision.HIGHEST

def complex_product(left, right):
    real_part = jnp.dot(left[0].astype(jnp.float32), right[0].astype(jnp.float32), precision=HIGHEST_PRECISION, preferred_element_type=jnp.float32) - jnp.dot(left[1].astype(jnp.float32), right[1].astype(jnp.float32), precision=HIGHEST_PRECISION, preferred_element_type=jnp.float32)
    imag_part = jnp.dot(left[0].astype(jnp.float32), right[1].astype(jnp.float32), precision=HIGHEST_PRECISION, preferred_element_type=jnp.float32) + jnp.dot(left[1].astype(jnp.float32), right[0].astype(jnp.float32), precision=HIGHEST_PRECISION, preferred_element_type=jnp.float32)
    return jnp.stack([real_part, imag_part])

def adjoint(matrix):
    return jnp.stack([matrix[0].T, -matrix[1].T])

def block_solve(system, rhs_block):
    order = system.shape[1]
    stacked = jnp.concatenate([jnp.concatenate([system[0], -system[1]], 1), jnp.concatenate([system[1], system[0]], 1)], 0)
    solved = jnp.linalg.solve(stacked, jnp.concatenate([rhs_block[0], rhs_block[1]], 0))
    return jnp.stack([solved[:order], solved[order:]])

def filter_point(diag_blocks, couplings, rhs_all, zeta_re, zeta_im):
    identity = jnp.eye(B, dtype=jnp.float32)
    carried = jnp.zeros((2, B, B + MCOL), jnp.float32)
    factors_all = []
    for layer in range(LAYERS):
        if layer < LAYERS - 1:
            link = couplings[layer]
        else:
            link = jnp.zeros((2, B, B), jnp.float32)
        schur = jnp.stack([zeta_re * identity - diag_blocks[layer, 0], zeta_im * identity - diag_blocks[layer, 1]]) - carried[:, :, :B]
        loaded = rhs_all[layer] + carried[:, :, B:]
        factors = block_solve(schur, jnp.concatenate([link, loaded], 2))
        factors_all.append(factors)
        carried = complex_product(adjoint(link), factors)
    current = jnp.zeros((2, B, MCOL), jnp.float32)
    layers_out = []
    for layer in range(LAYERS - 1, -1, -1):
        factors = factors_all[layer]
        current = factors[:, :, B:] + complex_product(factors[:, :, :B], current)
        layers_out.insert(0, current)
    return jnp.stack(layers_out)

def reference(diag_blocks, couplings, subspace, widths, owner_order, centers, radii):

    def one_window(item):
        rhs_all, width_one, center, radius = item
        live = (jnp.arange(MCOL, dtype=jnp.int32) < width_one).astype(jnp.float32)
        rhs_all = rhs_all * live

        def one_point(point_number):
            angle = 2.0 * math.pi * (point_number.astype(jnp.float32) + 0.5) / N_POINT
            zeta_re = center + radius * jnp.cos(angle)
            zeta_im = radius * jnp.sin(angle)
            solved = filter_point(diag_blocks, couplings, rhs_all, zeta_re, zeta_im)
            weight_re = radius * jnp.cos(angle) / N_POINT
            weight_im = radius * jnp.sin(angle) / N_POINT
            return jnp.stack([weight_re * solved[:, 0] - weight_im * solved[:, 1], weight_re * solved[:, 1] + weight_im * solved[:, 0]], axis=1)
        return jnp.sum(lax.map(one_point, jnp.arange(N_POINT, dtype=jnp.int32)), axis=0)
    window_sums = lax.map(one_window, (subspace, widths, centers, radii))
    return jnp.take(window_sums, owner_order, axis=0)
```

```python
import math

import jax
import jax.numpy as jnp
from jax import lax
from jax.experimental import pallas as pl
from jax.experimental.pallas import tpu as pltpu
from jax.sharding import PartitionSpec as P

F32 = jnp.float32
BF16 = jnp.bfloat16
COARSE = 0.1


def dot(left, right):
    return lax.dot_general(left, right, (((1,), (0,)), ((), ())), preferred_element_type=F32)


def hi_lo(value):
    high = value.astype(BF16)
    return high, (value - high.astype(F32)).astype(BF16)


def packed_pair(value):
    high, low = hi_lo(value)
    return jnp.concatenate([high, low], 1)


def left_triple(pair):
    half = pair.shape[1] // 2
    return jnp.concatenate([pair, pair[:, :half]], 1)


def embed(re, im):
    return jnp.concatenate([jnp.concatenate([re, im], 1), jnp.concatenate([-im, re], 1)], 0)


def embed_triple(re, im):
    re_high, re_low = hi_lo(re)
    im_high, im_low = hi_lo(im)
    high = embed(re_high, im_high)
    return jnp.concatenate([high, high, embed(re_low, im_low)], 0)


def times_i(value):
    half = value.shape[1] // 2
    return jnp.concatenate([-value[:, half:], value[:, :half]], 1)


def column_triple(value):
    high, low = hi_lo(jnp.concatenate([value, times_i(value)], 0))
    return jnp.concatenate([high, high, low], 0)


def eye_of(order):
    row = lax.broadcasted_iota(jnp.int32, (order, order), 0)
    col = lax.broadcasted_iota(jnp.int32, (order, order), 1)
    return (row == col).astype(F32)


def invert(s_re, s_im, zeta_im, s_emb, x_ref, work):
    n = s_re.shape[0]
    eye = eye_of(n)
    s_emb[...] = embed_triple(s_re, s_im)
    adj_re, adj_im = s_re.T, -s_im.T
    gram = dot(jnp.concatenate([adj_re, adj_im], 1).astype(BF16), s_emb[0 : 2 * n, :])
    sums = jnp.sum(jnp.abs(gram), 0, keepdims=True)
    bound_sq = jnp.max(sums[:, :n] + sums[:, n:], axis=1, keepdims=True)
    bound = jnp.sqrt(bound_sq)
    ratio = jnp.abs(zeta_im) / bound
    shrink = 1.0 / (1.0 + ratio + ratio * ratio)
    alpha = shrink / bound_sq
    beta = shrink / bound * jnp.where(zeta_im > 0, 1.0, -1.0)
    x_re = alpha * adj_re
    x_im = alpha * adj_im - beta * eye
    x_ref[...] = jnp.concatenate([x_re, x_im], 1)
    work[:, 0 : 2 * n] = embed(
        eye - alpha * gram[:, :n] - beta * s_im, beta * s_re - alpha * gram[:, n:]
    ).astype(BF16)
    work[:, 2 * n :] = embed(x_re, x_im).astype(BF16)

    def double(size):
        both = dot(work[0:n, 0 : 2 * n], work[...])
        work[:, 0 : 2 * n] = embed(both[:, :n], both[:, n : 2 * n]).astype(BF16)
        x_now = x_ref[...] + both[:, 2 * n :]
        x_ref[...] = x_now
        work[:, 2 * n :] = embed(x_now[:, :n], x_now[:, n:]).astype(BF16)
        return size * size

    lax.while_loop(lambda size: size > COARSE, double, shrink[0, 0])
    wide_eye = jnp.concatenate([eye, jnp.zeros((n, n), F32)], 1)
    rest = wide_eye - dot(work[0:n, 2 * n :], s_emb[0 : 2 * n, :])
    x_ref[...] = x_ref[...] + dot(rest.astype(BF16), work[:, 2 * n :])
    x_now = x_ref[...]
    rest = wide_eye - dot(left_triple(packed_pair(x_now)), s_emb[...])
    return x_now + dot(rest.astype(BF16), embed(x_now[:, :n], x_now[:, n:]).astype(BF16))


def pick(flag, if_true, if_false):
    return jnp.where(flag, if_true, if_false)


def rows_of(direct, swapped, plane, point):
    mine, other = direct[plane], swapped[plane]
    return jnp.concatenate([pick(point == 0, mine, other), pick(point == 0, other, mine)], 0)


def unpack_diag(packed):
    n = packed.shape[0]
    row = lax.broadcasted_iota(jnp.int32, (n, n), 0)
    col = lax.broadcasted_iota(jnp.int32, (n, n), 1)
    turned = packed.T
    re = jnp.where(row >= col, packed, turned)
    im = jnp.where(row < col, packed, jnp.where(row > col, -turned, 0.0))
    return re, im


def oriented(flag, here, there):
    re = pick(flag, here[0], there[0].T)
    im = pick(flag, here[1], -there[1].T)
    adj_re = pick(flag, here[0].T, there[0])
    adj_im = pick(flag, -here[1].T, there[1])
    return re, im, adj_re, adj_im


def slot_of(scal, owner, slab, dims):
    win_count, local_count, parts = dims
    window = owner[scal[0] * local_count + slab // parts]
    shift = lax.rem(scal[0] - window // local_count + win_count, win_count)
    return shift, lax.rem(window, local_count)


def look_up(tables, row, shift, index):
    value = tables[0][row, index]
    for k in range(1, len(tables)):
        value = jnp.where(shift == k, tables[k][row, index], value)
    return value


def contour(scal, owner, tables, dims, point_count):
    shift, index = slot_of(scal, owner, scal[1], dims)
    center = look_up(tables, 0, shift, index)
    radius = look_up(tables, 1, shift, index)
    cosine = jnp.float32(0.0)
    sine = jnp.float32(0.0)
    for p in range(point_count):
        angle = 2.0 * math.pi * (p + 0.5) / point_count
        cosine = jnp.where(scal[2] == p, jnp.float32(math.cos(angle)), cosine)
        sine = jnp.where(scal[2] == p, jnp.float32(math.sin(angle)), sine)
    return center + radius * cosine, radius * sine, radius * cosine / point_count, radius * sine / point_count


def per_device(diag_blocks, couplings, subspace, widths, owner_order, centers, radii):
    slab = lax.axis_index("slab")
    slab_count = lax.axis_size("slab")
    point = lax.axis_index("point")
    point_count = lax.axis_size("point")
    win = lax.axis_index("win")
    win_count = lax.axis_size("win")
    n = diag_blocks.shape[2]
    columns = subspace.shape[4]
    local_count = subspace.shape[0]
    parts = slab_count // local_count
    width = columns // parts
    lanes = 2 * width
    half = n // point_count
    dims = (win_count, local_count, parts)
    assert slab_count == 4 and point_count == 2 and parts == 2

    smem = pl.BlockSpec(memory_space=pltpu.SMEM)
    vmem = pl.BlockSpec(memory_space=pltpu.VMEM)
    grant = pltpu.CompilerParams(vmem_limit_bytes=56 * 1024 * 1024)
    pair_shape = jax.ShapeDtypeStruct((n, 4 * n), BF16)
    scratch = [
        pltpu.VMEM((6 * n, 2 * n), BF16),
        pltpu.VMEM((n, 2 * n), F32),
        pltpu.VMEM((2 * n, 4 * n), BF16),
    ]

    def exchange(value, distance):
        return lax.ppermute(value, "slab", [(i, i ^ distance) for i in range(slab_count)])

    def swap(value):
        return lax.ppermute(value, "point", [(i, i ^ 1) for i in range(point_count)])

    def along_win(value, shift):
        return lax.ppermute(value, "win", [(i, (i + shift) % win_count) for i in range(win_count)])

    scal = jnp.stack([win, slab, point]).astype(jnp.int32)
    table = jnp.stack([centers, radii, widths.astype(F32)])
    row = lax.broadcasted_iota(jnp.int32, (n, n), 0)
    col = lax.broadcasted_iota(jnp.int32, (n, n), 1)
    packed = jnp.where(row >= col, diag_blocks[0, 0], diag_blocks[0, 1])
    shard = jnp.concatenate([packed[None], couplings[0]], 0)
    carried = lax.dynamic_slice_in_dim(shard, point * half, half, 1)
    from_x = exchange(carried, 1)
    from_y = exchange(carried, 2)
    tables = [table] + [along_win(table, k) for k in range(1, win_count)]
    block = lax.dynamic_slice_in_dim(subspace[:, 0], point * half, half, 2)
    blocks = [block] + [along_win(block, k) for k in range(1, win_count)]
    relay = jnp.where(point == 0, from_y, from_x)
    flat = [(2 * s, 2 * (s ^ 1)) for s in range(slab_count)]
    flat += [(2 * s + 1, 2 * (s ^ 2) + 1) for s in range(slab_count)]
    from_far = lax.ppermute(relay, ("slab", "point"), flat)
    from_x = (from_x, swap(from_x))
    from_y = (from_y, swap(from_y))
    from_far = (from_far, swap(from_far))

    def first_body(*refs):
        scal, owner = refs[:2]
        tables = refs[2 : 2 + win_count]
        diag, x_out, s_emb, x_ref, work = refs[2 + win_count :]
        z_re, z_im, _, _ = contour(scal, owner, tables, dims, point_count)
        eye = eye_of(n)
        x_out[...] = packed_pair(
            invert(z_re * eye - diag[0, 0], z_im * eye - diag[0, 1], z_im, s_emb, x_ref, work)
        )

    head = [scal, owner_order] + tables
    head_specs = [smem] * len(head)
    x_own = pl.pallas_call(
        first_body,
        out_shape=pair_shape,
        in_specs=head_specs + [vmem],
        out_specs=vmem,
        scratch_shapes=scratch,
        compiler_params=grant,
    )(*head, diag_blocks)

    def second_body(*refs):
        scal, owner = refs[:2]
        tables = refs[2 : 2 + win_count]
        (x_own, own_c, x_dir, x_swp, x_out, w_out, l_out, s_emb, x_ref, work) = refs[2 + win_count :]
        z_re, z_im, _, _ = contour(scal, owner, tables, dims, point_count)
        p = scal[2]
        near = [rows_of(x_dir, x_swp, k, p) for k in range(3)]
        even = lax.rem(scal[1], 2) == 0
        re, im, adj_re, adj_im = oriented(even, (own_c[0, 0], own_c[0, 1]), (near[1], near[2]))
        solved = dot(left_triple(x_own[...]), embed_triple(re, im))
        w_out[...] = packed_pair(solved)
        left = packed_pair(jnp.concatenate([adj_re, adj_im], 1))
        l_out[...] = left
        update = dot(left_triple(left), embed_triple(solved[:, :n], solved[:, n:]))
        d_re, d_im = unpack_diag(near[0])
        eye = eye_of(n)
        x_out[...] = packed_pair(
            invert(
                z_re * eye - d_re - update[:, :n],
                z_im * eye - d_im - update[:, n:],
                z_im,
                s_emb,
                x_ref,
                work,
            )
        )

    x_near, w_near, l_near = pl.pallas_call(
        second_body,
        out_shape=[pair_shape] * 3,
        in_specs=head_specs + [vmem] * 4,
        out_specs=[vmem] * 3,
        scratch_shapes=scratch,
        compiler_params=grant,
    )(*head, x_own, couplings, *from_x)

    def third_body(*refs):
        scal, owner = refs[:2]
        tables = refs[2 : 2 + win_count]
        (x_near, x_dir, x_swp, y_dir, y_swp, x_out, w_out, l_out, s_emb, x_ref, work, s_ref) = refs[
            2 + win_count :
        ]
        z_re, z_im, _, _ = contour(scal, owner, tables, dims, point_count)
        p = scal[2]
        even = lax.rem(scal[1], 2) == 0
        chain = lax.rem(scal[1], 2) == scal[1] // 2
        d_re, d_im = unpack_diag(rows_of(y_dir, y_swp, 0, p))
        eye = eye_of(n)
        s_ref[...] = jnp.concatenate([z_re * eye - d_re, z_im * eye - d_im], 1)

        @pl.when(chain)
        def _():
            re, im, adj_re, adj_im = oriented(
                even,
                [rows_of(x_dir, x_swp, k, p) for k in (1, 2)],
                [rows_of(y_dir, y_swp, k, p) for k in (1, 2)],
            )
            solved = dot(left_triple(x_near[...]), embed_triple(re, im))
            w_out[...] = packed_pair(solved)
            left = packed_pair(jnp.concatenate([adj_re, adj_im], 1))
            l_out[...] = left
            s_ref[...] = s_ref[...] - dot(
                left_triple(left), embed_triple(solved[:, :n], solved[:, n:])
            )

        x_out[...] = packed_pair(invert(s_ref[:, :n], s_ref[:, n:], z_im, s_emb, x_ref, work))

    x_side, w_mid, l_mid = pl.pallas_call(
        third_body,
        out_shape=[pair_shape] * 3,
        in_specs=head_specs + [vmem] * 5,
        out_specs=[vmem] * 3,
        scratch_shapes=scratch + [pltpu.VMEM((n, 2 * n), F32)],
        compiler_params=grant,
    )(*head, x_near, *from_x, *from_y)

    def route_body(*refs):
        scal, owner = refs[:2]
        tables = refs[2 : 2 + win_count]
        blocks = refs[2 + win_count : 2 + 2 * win_count]
        outs = refs[2 + 2 * win_count :]
        lane = lax.broadcasted_iota(jnp.int32, (half, lanes), 1)
        for k in range(slab_count):
            target = scal[1] ^ k
            part = lax.rem(target, parts)
            shift, index = slot_of(scal, owner, target, dims)
            live = look_up(tables, 2, shift, index).astype(jnp.int32)
            for k_win in range(win_count):

                @pl.when(shift == k_win)
                def _():
                    re = blocks[k_win][index, 0]
                    im = blocks[k_win][index, 1]
                    mine = jnp.where(
                        part == 0,
                        jnp.where(lane < width, re, pltpu.roll(im, width, 1)),
                        jnp.where(lane < width, pltpu.roll(re, width, 1), im),
                    )
                    number = part * width + lax.rem(lane, width)
                    outs[k][...] = jnp.where(number < live, mine, 0.0)

    piece = jax.ShapeDtypeStruct((half, lanes), F32)
    routed = pl.pallas_call(
        route_body,
        out_shape=[piece] * slab_count,
        in_specs=head_specs + [vmem] * win_count,
        out_specs=[vmem] * slab_count,
        compiler_params=grant,
    )(*head, *blocks)
    rhs = jnp.stack([routed[0]] + [exchange(routed[k], k) for k in range(1, slab_count)])
    rhs = (rhs, swap(rhs))

    def fourth_body(*refs):
        scal, owner = refs[:2]
        tables = refs[2 : 2 + win_count]
        (x_own, x_near, x_side, w_near, l_near, w_mid, l_mid, own_c, y_dir, y_swp, f_dir, f_swp) = refs[
            2 + win_count : 14 + win_count
        ]
        (x_out, w_far, l_far, w_cross, l_cross, w_last, l_last, s_emb, x_ref, work, s_ref) = refs[
            14 + win_count :
        ]
        z_re, z_im, _, _ = contour(scal, owner, tables, dims, point_count)
        p = scal[2]
        even = lax.rem(scal[1], 2) == 0
        chain = lax.rem(scal[1], 2) == scal[1] // 2
        far = [rows_of(f_dir, f_swp, k, p) for k in range(3)]
        side = [rows_of(y_dir, y_swp, k, p) for k in (1, 2)]
        d_re, d_im = unpack_diag(far[0])
        eye = eye_of(n)
        s_ref[...] = jnp.concatenate([z_re * eye - d_re, z_im * eye - d_im], 1)

        @pl.when(chain)
        def _():
            zero = jnp.zeros((n, 4 * n), BF16)
            w_cross[...] = zero
            l_cross[...] = zero
            w_far[...] = w_mid[...]
            l_far[...] = l_mid[...]

        @pl.when(jnp.logical_not(chain))
        def _():
            odd = jnp.logical_not(even)
            re, im, adj_re, adj_im = oriented(odd, (own_c[0, 0], own_c[0, 1]), (far[1], far[2]))
            cross = dot(left_triple(x_own[...]), embed_triple(re, im))
            w_cross[...] = packed_pair(cross)
            left = packed_pair(jnp.concatenate([adj_re, adj_im], 1))
            l_cross[...] = left
            cross_emb = embed_triple(cross[:, :n], cross[:, n:])
            fill = dot(left_triple(l_near[...]), cross_emb)
            w_pair = w_near[...]
            high, low = w_pair[:, : 2 * n], w_pair[:, 2 * n :]
            near_high = embed(high[:, :n], high[:, n:])
            near_emb = jnp.concatenate([near_high, near_high, embed(low[:, :n], low[:, n:])], 0)
            both = dot(left_triple(left), jnp.concatenate([near_emb, cross_emb], 1))
            back = packed_pair(both[:, : 2 * n])
            l_far[...] = back
            solved = dot(left_triple(x_near[...]), embed_triple(fill[:, :n], fill[:, n:]))
            w_far[...] = packed_pair(solved)
            s_ref[...] = (
                s_ref[...]
                - both[:, 2 * n :]
                - dot(left_triple(back), embed_triple(solved[:, :n], solved[:, n:]))
            )

        re, im, adj_re, adj_im = oriented(even, side, (far[1], far[2]))
        solved = dot(left_triple(x_side[...]), embed_triple(re, im))
        w_last[...] = packed_pair(solved)
        left = packed_pair(jnp.concatenate([adj_re, adj_im], 1))
        l_last[...] = left
        s_now = s_ref[...] - dot(left_triple(left), embed_triple(solved[:, :n], solved[:, n:]))
        x_out[...] = packed_pair(invert(s_now[:, :n], s_now[:, n:], z_im, s_emb, x_ref, work))

    x_far, w_far, l_far, w_cross, l_cross, w_last, l_last = pl.pallas_call(
        fourth_body,
        out_shape=[pair_shape] * 7,
        in_specs=head_specs + [vmem] * 12,
        out_specs=[vmem] * 7,
        scratch_shapes=scratch + [pltpu.VMEM((n, 2 * n), F32)],
        compiler_params=grant,
    )(*head, x_own, x_near, x_side, w_near, l_near, w_mid, l_mid, couplings, *from_y, *from_far)

    def solve_body(*refs):
        scal, owner = refs[:2]
        tables = refs[2 : 2 + win_count]
        (x_own, x_near, x_side, x_far, w_near, l_near, w_cross, l_cross, w_far, l_far, w_last, l_last) = refs[
            2 + win_count : 14 + win_count
        ]
        b_dir, b_swp, keep, send = refs[14 + win_count :]
        _, _, weight_re, weight_im = contour(scal, owner, tables, dims, point_count)
        p = scal[2]
        chain = lax.rem(scal[1], 2) == scal[1] // 2

        def apply(ref, value):
            return dot(left_triple(ref[...]), column_triple(value))

        b_own, b_near, b_side, b_far = [rows_of(b_dir, b_swp, k, p) for k in range(4)]
        u_own = apply(x_own, b_own)
        b_near = b_near + apply(l_near, u_own)
        b_far = b_far + apply(l_cross, u_own)
        u_near = apply(x_near, b_near)
        step = apply(l_far, u_near)
        b_side = b_side + pick(chain, step, 0.0)
        b_far = b_far + pick(chain, 0.0, step)
        u_side = apply(x_side, b_side)
        b_far = b_far + apply(l_last, u_side)
        far = apply(x_far, b_far)
        side = u_side + apply(w_last, far)
        near = u_near + apply(w_far, pick(chain, side, far))
        own = u_own + apply(w_near, near) + apply(w_cross, far)
        for k, value in enumerate((own, near, side, far)):
            value = weight_re * value + weight_im * times_i(value)
            keep[k] = pick(p == 0, value[:half], value[half:])
            send[k] = pick(p == 0, value[half:], value[:half])

    quad = jax.ShapeDtypeStruct((slab_count, half, lanes), F32)
    keep, send = pl.pallas_call(
        solve_body,
        out_shape=[quad] * 2,
        in_specs=head_specs + [vmem] * 14,
        out_specs=[vmem] * 2,
        compiler_params=grant,
    )(
        *head, x_own, x_near, x_side, x_far, w_near, l_near, w_cross, l_cross, w_far, l_far, w_last, l_last, *rhs
    )
    total = keep + swap(send)
    shares = [total[0]] + [exchange(total[k], k) for k in range(1, slab_count)]

    def place_body(*refs):
        scal = refs[0]
        shares = refs[1 : 1 + slab_count]
        out = refs[1 + slab_count]
        lane = lax.broadcasted_iota(jnp.int32, (half, lanes), 1)
        for slot in range(local_count):
            found = []
            for part in range(parts):
                distance = scal[1] ^ (slot * parts + part)
                value = shares[0][...]
                for k in range(1, slab_count):
                    value = jnp.where(distance == k, shares[k][...], value)
                found.append(value)
            low, high = found
            out[slot, 0, 0] = jnp.where(lane < width, low, pltpu.roll(high, width, 1))
            out[slot, 0, 1] = jnp.where(lane < width, pltpu.roll(low, width, 1), high)

    return pl.pallas_call(
        place_body,
        out_shape=jax.ShapeDtypeStruct((local_count, 1, 2, half, columns), F32),
        in_specs=[smem] + [vmem] * slab_count,
        out_specs=vmem,
        compiler_params=grant,
    )(scal, *shares)


def solution(mesh):
    placed = (
        P("slab", None, None, None),
        P("slab", None, None, None),
        P("win", "slab", None, None, None),
        P("win"),
        P(),
        P("win"),
        P("win"),
    )
    return jax.shard_map(
        per_device,
        mesh=mesh,
        in_specs=placed,
        out_specs=P("win", "slab", None, "point", None),
        check_vma=False,
    )
```

```python
import math

import jax
import jax.numpy as jnp
from jax import lax
from jax.experimental import pallas as pl
from jax.experimental.pallas import tpu as pltpu
from jax.sharding import PartitionSpec as P


F32 = jnp.float32
BF16 = jnp.bfloat16
COARSE = 0.1


def dot(left, right):
    return lax.dot_general(left, right, (((1,), (0,)), ((), ())), preferred_element_type=F32)


def hi_lo(value):
    high = value.astype(BF16)
    return high, (value - high.astype(F32)).astype(BF16)


def packed_pair(value):
    high, low = hi_lo(value)
    return jnp.concatenate([high, low], 1)


def left_triple(pair):
    half = pair.shape[1] // 2
    return jnp.concatenate([pair, pair[:, :half]], 1)


def embed(re, im):
    return jnp.concatenate([jnp.concatenate([re, im], 1), jnp.concatenate([-im, re], 1)], 0)


def embed_triple(re, im):
    re_high, re_low = hi_lo(re)
    im_high, im_low = hi_lo(im)
    high = embed(re_high, im_high)
    return jnp.concatenate([high, high, embed(re_low, im_low)], 0)


def times_i(value):
    half = value.shape[1] // 2
    return jnp.concatenate([-value[:, half:], value[:, :half]], 1)


def column_triple(value):
    high, low = hi_lo(jnp.concatenate([value, times_i(value)], 0))
    return jnp.concatenate([high, high, low], 0)


def lasting(micros):
    return pl.CostEstimate(flops=micros * 10**9, transcendentals=0, bytes_accessed=micros * 10**6)


def eye_of(order):
    row = lax.broadcasted_iota(jnp.int32, (order, order), 0)
    col = lax.broadcasted_iota(jnp.int32, (order, order), 1)
    return (row == col).astype(F32)


def invert(s_re, s_im, zeta_im, s_emb, x_ref, work):
    n = s_re.shape[0]
    eye = eye_of(n)
    s_emb[...] = embed_triple(s_re, s_im)
    adj_re, adj_im = s_re.T, -s_im.T
    gram = dot(jnp.concatenate([adj_re, adj_im], 1).astype(BF16), s_emb[0 : 2 * n, :])
    sums = jnp.sum(jnp.abs(gram), 0, keepdims=True)
    bound_sq = jnp.max(sums[:, :n] + sums[:, n:], axis=1, keepdims=True)
    bound = jnp.sqrt(bound_sq)
    ratio = jnp.abs(zeta_im) / bound
    shrink = 1.0 / (1.0 + ratio + ratio * ratio)
    alpha = shrink / bound_sq
    beta = shrink / bound * jnp.where(zeta_im > 0, 1.0, -1.0)
    x_re = alpha * adj_re
    x_im = alpha * adj_im - beta * eye
    x_ref[...] = jnp.concatenate([x_re, x_im], 1)
    work[:, 0 : 2 * n] = embed(
        eye - alpha * gram[:, :n] - beta * s_im, beta * s_re - alpha * gram[:, n:]
    ).astype(BF16)
    work[:, 2 * n :] = embed(x_re, x_im).astype(BF16)

    def double(size):
        both = dot(work[0:n, 0 : 2 * n], work[...])
        work[:, 0 : 2 * n] = embed(both[:, :n], both[:, n : 2 * n]).astype(BF16)
        x_now = x_ref[...] + both[:, 2 * n :]
        x_ref[...] = x_now
        work[:, 2 * n :] = embed(x_now[:, :n], x_now[:, n:]).astype(BF16)
        return size * size

    lax.while_loop(lambda size: size > COARSE, double, shrink[0, 0])
    wide_eye = jnp.concatenate([eye, jnp.zeros((n, n), F32)], 1)
    rest = wide_eye - dot(work[0:n, 2 * n :], s_emb[0 : 2 * n, :])
    x_ref[...] = x_ref[...] + dot(rest.astype(BF16), work[:, 2 * n :])
    x_now = x_ref[...]
    rest = wide_eye - dot(left_triple(packed_pair(x_now)), s_emb[...])
    return x_now + dot(rest.astype(BF16), embed(x_now[:, :n], x_now[:, n:]).astype(BF16))


def pick(flag, if_true, if_false):
    return jnp.where(flag, if_true, if_false)


def rows_of(direct, swapped, plane, point):
    mine, other = direct[plane], swapped[plane]
    return jnp.concatenate([pick(point == 0, mine, other), pick(point == 0, other, mine)], 0)


def unpack_diag(packed):
    n = packed.shape[0]
    row = lax.broadcasted_iota(jnp.int32, (n, n), 0)
    col = lax.broadcasted_iota(jnp.int32, (n, n), 1)
    turned = packed.T
    re = jnp.where(row >= col, packed, turned)
    im = jnp.where(row < col, packed, jnp.where(row > col, -turned, 0.0))
    return re, im


def oriented(flag, here, there):
    re = pick(flag, here[0], there[0].T)
    im = pick(flag, here[1], -there[1].T)
    adj_re = pick(flag, here[0].T, there[0])
    adj_im = pick(flag, -here[1].T, there[1])
    return re, im, adj_re, adj_im


def position():
    return lax.axis_index("win"), lax.axis_index("slab"), lax.axis_index("point")


def slot_of(scal, owner, slab, dims):
    local_count, parts = dims
    window = owner[scal[0] * local_count + slab // parts]
    return scal[0] ^ (window // local_count), lax.rem(window, local_count)


def look_up(tables, row, shift, index):
    value = tables[0][row, index]
    for k in range(1, len(tables)):
        value = jnp.where(shift == k, tables[k][row, index], value)
    return value


def contour(scal, owner, tables, dims, point_count):
    shift, index = slot_of(scal, owner, scal[1], dims)
    center = look_up(tables, 0, shift, index)
    radius = look_up(tables, 1, shift, index)
    cosine = jnp.float32(0.0)
    sine = jnp.float32(0.0)
    for p in range(point_count):
        angle = 2.0 * math.pi * (p + 0.5) / point_count
        cosine = jnp.where(scal[2] == p, jnp.float32(math.cos(angle)), cosine)
        sine = jnp.where(scal[2] == p, jnp.float32(math.sin(angle)), sine)
    return center + radius * cosine, radius * sine, radius * cosine / point_count, radius * sine / point_count


def per_device(diag_blocks, couplings, subspace, widths, owner_order, centers, radii):
    slab_count = lax.axis_size("slab")
    point_count = lax.axis_size("point")
    win_count = lax.axis_size("win")
    n = diag_blocks.shape[2]
    columns = subspace.shape[4]
    local_count = subspace.shape[0]
    parts = slab_count // local_count
    width = columns // parts
    lanes = 2 * width
    half = n // point_count
    dims = (local_count, parts)
    assert slab_count == 4 and point_count == 2 and parts == 2
    assert win_count & (win_count - 1) == 0

    smem = pl.BlockSpec(memory_space=pltpu.SMEM)
    vmem = pl.BlockSpec(memory_space=pltpu.VMEM)
    grant = pltpu.CompilerParams(vmem_limit_bytes=20 * 1024 * 1024)
    pair_shape = jax.ShapeDtypeStruct((n, 4 * n), BF16)
    scratch = [
        pltpu.VMEM((6 * n, 2 * n), BF16),
        pltpu.VMEM((n, 2 * n), F32),
        pltpu.VMEM((2 * n, 4 * n), BF16),
    ]

    def exchange(value, distance):
        return lax.ppermute(value, "slab", [(i, i ^ distance) for i in range(slab_count)])

    def swap(value):
        return lax.ppermute(value, "point", [(i, i ^ 1) for i in range(point_count)])

    def along_win(value, shift):
        return lax.ppermute(value, "win", [(i, i ^ shift) for i in range(win_count)])

    table = jnp.stack([centers, radii])
    tables = [table]
    for k in range(1, win_count):
        tables.append(along_win(table, k))

    def prepare_body(widths, diag, links, vectors, carried, block, pair, sems):
        start = position()[2] * half
        rows = pl.ds(start, half)
        moves = [pltpu.make_async_copy(diag.at[0, :, rows, :], pair, sems.at[0])]
        moves.append(pltpu.make_async_copy(links.at[0, :, rows, :], carried.at[pl.ds(1, 2)], sems.at[1]))
        moves.append(pltpu.make_async_copy(vectors.at[:, 0, :, rows, :], block, sems.at[2]))
        for move in moves:
            move.start()
        for move in moves:
            move.wait()
        row = lax.broadcasted_iota(jnp.int32, (half, n), 0) + start
        col = lax.broadcasted_iota(jnp.int32, (half, n), 1)
        carried[0] = jnp.where(row >= col, pair[0], pair[1])
        number = lax.broadcasted_iota(jnp.int32, (half, columns), 1)
        for j in range(local_count):
            for k in range(2):
                block[j, k] = jnp.where(number < widths[j], block[j, k], 0.0)

    anywhere = pl.BlockSpec(memory_space=pltpu.HBM)
    prepare = pl.pallas_call(
        prepare_body,
        out_shape=[
            jax.ShapeDtypeStruct((3, half, n), F32),
            jax.ShapeDtypeStruct((local_count, 2, half, columns), F32),
        ],
        in_specs=[smem] + [anywhere] * 3,
        out_specs=[vmem] * 2,
        scratch_shapes=[pltpu.VMEM((2, half, n), F32), pltpu.SemaphoreType.DMA((3,))],
        compiler_params=grant,
    )
    carried, block = prepare(widths, diag_blocks, couplings, subspace)
    from_x = exchange(carried, 1)
    from_y = exchange(carried, 2)
    blocks = [block]
    for k in range(1, win_count):
        blocks.append(along_win(block, k))

    def first_body(*refs):
        scal, owner = position(), refs[0]
        tables = refs[1 : 1 + win_count]
        diag, x_out, prm, s_emb, x_ref, work = refs[1 + win_count :]
        z_re, z_im, weight_re, weight_im = contour(scal, owner, tables, dims, point_count)
        for k, value in enumerate((z_re, z_im, weight_re, weight_im)):
            prm[k] = value
        eye = eye_of(n)
        x_out[...] = packed_pair(
            invert(z_re * eye - diag[0, 0], z_im * eye - diag[0, 1], z_im, s_emb, x_ref, work)
        )

    head = [owner_order] + tables
    head_specs = [smem] * len(head)
    first = pl.pallas_call(
        first_body,
        out_shape=[pair_shape, jax.ShapeDtypeStruct((4,), F32)],
        in_specs=head_specs + [vmem],
        out_specs=[vmem, smem],
        scratch_shapes=scratch,
        cost_estimate=lasting(6),
        compiler_params=grant,
    )
    x_own, prm = first(*head, diag_blocks)

    relay = jnp.where(lax.axis_index("point") == 0, from_y, from_x)
    flat = [(2 * s, 2 * (s ^ 1)) for s in range(slab_count)]
    flat += [(2 * s + 1, 2 * (s ^ 2) + 1) for s in range(slab_count)]
    from_far = lax.ppermute(relay, ("slab", "point"), flat)
    from_x = (from_x, swap(from_x))
    from_y = (from_y, swap(from_y))
    from_far = (from_far, swap(from_far))

    def second_body(*refs):
        scal, prm = position(), refs[0]
        (x_own, own_c, x_dir, x_swp, x_out, w_out, l_out, s_emb, x_ref, work) = refs[1:]
        z_re, z_im = prm[0], prm[1]
        p = scal[2]
        near = [rows_of(x_dir, x_swp, k, p) for k in range(3)]
        even = lax.rem(scal[1], 2) == 0
        re, im, adj_re, adj_im = oriented(even, (own_c[0, 0], own_c[0, 1]), (near[1], near[2]))
        solved = dot(left_triple(x_own[...]), embed_triple(re, im))
        w_out[...] = packed_pair(solved)
        left = packed_pair(jnp.concatenate([adj_re, adj_im], 1))
        l_out[...] = left
        update = dot(left_triple(left), embed_triple(solved[:, :n], solved[:, n:]))
        d_re, d_im = unpack_diag(near[0])
        eye = eye_of(n)
        x_out[...] = packed_pair(
            invert(
                z_re * eye - d_re - update[:, :n],
                z_im * eye - d_im - update[:, n:],
                z_im,
                s_emb,
                x_ref,
                work,
            )
        )

    second = pl.pallas_call(
        second_body,
        out_shape=[pair_shape] * 3,
        in_specs=[smem] + [vmem] * 4,
        out_specs=[vmem] * 3,
        scratch_shapes=scratch,
        cost_estimate=lasting(8),
        compiler_params=grant,
    )
    x_near, w_near, l_near = second(prm, x_own, couplings, *from_x)

    def third_body(*refs):
        scal, prm = position(), refs[0]
        (x_near, x_dir, x_swp, y_dir, y_swp, x_out, w_out, l_out, later) = refs[1:10]
        s_emb, x_ref, work, s_ref = refs[10:]
        for k in range(4):
            later[k] = prm[k]
        z_re, z_im = prm[0], prm[1]
        p = scal[2]
        even = lax.rem(scal[1], 2) == 0
        chain = lax.rem(scal[1], 2) == scal[1] // 2
        d_re, d_im = unpack_diag(rows_of(y_dir, y_swp, 0, p))
        eye = eye_of(n)
        s_ref[...] = jnp.concatenate([z_re * eye - d_re, z_im * eye - d_im], 1)

        @pl.when(chain)
        def _():
            re, im, adj_re, adj_im = oriented(
                even,
                [rows_of(x_dir, x_swp, k, p) for k in (1, 2)],
                [rows_of(y_dir, y_swp, k, p) for k in (1, 2)],
            )
            solved = dot(left_triple(x_near[...]), embed_triple(re, im))
            w_out[...] = packed_pair(solved)
            left = packed_pair(jnp.concatenate([adj_re, adj_im], 1))
            l_out[...] = left
            s_ref[...] = s_ref[...] - dot(
                left_triple(left), embed_triple(solved[:, :n], solved[:, n:])
            )

        x_out[...] = packed_pair(invert(s_ref[:, :n], s_ref[:, n:], z_im, s_emb, x_ref, work))

    x_side, w_mid, l_mid, later = pl.pallas_call(
        third_body,
        out_shape=[pair_shape] * 3 + [jax.ShapeDtypeStruct((4,), F32)],
        in_specs=[smem] + [vmem] * 5,
        out_specs=[vmem] * 3 + [smem],
        scratch_shapes=scratch + [pltpu.VMEM((n, 2 * n), F32)],
        cost_estimate=lasting(8),
        compiler_params=grant,
    )(prm, x_near, *from_x, *from_y)

    def route_body(*refs):
        scal, owner = position(), refs[0]
        blocks = refs[1 : 1 + win_count]
        out = refs[2 + win_count]
        lane = lax.broadcasted_iota(jnp.int32, (half, lanes), 1)
        for k in range(slab_count):
            target = scal[1] ^ k
            part = lax.rem(target, parts)
            shift, index = slot_of(scal, owner, target, dims)
            for k_win in range(win_count):

                @pl.when(shift == k_win)
                def _():
                    re = blocks[k_win][index, 0]
                    im = blocks[k_win][index, 1]
                    mine = jnp.where(
                        part == 0,
                        jnp.where(lane < width, re, pltpu.roll(im, width, 1)),
                        jnp.where(lane < width, pltpu.roll(re, width, 1), im),
                    )
                    out[k] = mine

    piece = jax.ShapeDtypeStruct((half, lanes), F32)
    quad = jax.ShapeDtypeStruct((slab_count, half, lanes), F32)
    routed = pl.pallas_call(
        route_body,
        out_shape=quad,
        in_specs=[smem] + [vmem] * win_count + [smem],
        out_specs=vmem,
        cost_estimate=lasting(2),
        compiler_params=grant,
    )(owner_order, *blocks, later)

    def join_body(mine, other, *outs):
        p = position()[2]
        for k in range(slab_count):
            outs[k][pl.ds(p * half, half), :] = mine[k]
            outs[k][pl.ds((1 - p) * half, half), :] = other[k]

    joined = pl.pallas_call(
        join_body,
        out_shape=[jax.ShapeDtypeStruct((n, lanes), F32)] * slab_count,
        in_specs=[vmem] * 2,
        out_specs=[vmem] * slab_count,
        compiler_params=grant,
    )(routed, swap(routed))
    rhs = [joined[0]] + [exchange(joined[k], k) for k in range(1, slab_count)]

    def fourth_body(*refs):
        scal, prm = position(), refs[0]
        (x_own, x_near, x_side, w_near, l_near, w_mid, l_mid, own_c, y_dir, y_swp, f_dir, f_swp) = refs[1:13]
        (x_out, w_far, l_far, w_cross, l_cross, w_last, l_last, s_emb, x_ref, work, s_ref) = refs[13:]
        z_re, z_im = prm[0], prm[1]
        p = scal[2]
        even = lax.rem(scal[1], 2) == 0
        chain = lax.rem(scal[1], 2) == scal[1] // 2
        far = [rows_of(f_dir, f_swp, k, p) for k in range(3)]
        side = [rows_of(y_dir, y_swp, k, p) for k in (1, 2)]
        d_re, d_im = unpack_diag(far[0])
        eye = eye_of(n)
        s_ref[...] = jnp.concatenate([z_re * eye - d_re, z_im * eye - d_im], 1)

        @pl.when(chain)
        def _():
            zero = jnp.zeros((n, 4 * n), BF16)
            w_cross[...] = zero
            l_cross[...] = zero
            w_far[...] = w_mid[...]
            l_far[...] = l_mid[...]

        @pl.when(jnp.logical_not(chain))
        def _():
            odd = jnp.logical_not(even)
            re, im, adj_re, adj_im = oriented(odd, (own_c[0, 0], own_c[0, 1]), (far[1], far[2]))
            cross = dot(left_triple(x_own[...]), embed_triple(re, im))
            w_cross[...] = packed_pair(cross)
            left = packed_pair(jnp.concatenate([adj_re, adj_im], 1))
            l_cross[...] = left
            cross_emb = embed_triple(cross[:, :n], cross[:, n:])
            fill = dot(left_triple(l_near[...]), cross_emb)
            w_pair = w_near[...]
            high, low = w_pair[:, : 2 * n], w_pair[:, 2 * n :]
            near_high = embed(high[:, :n], high[:, n:])
            near_emb = jnp.concatenate([near_high, near_high, embed(low[:, :n], low[:, n:])], 0)
            both = dot(left_triple(left), jnp.concatenate([near_emb, cross_emb], 1))
            back = packed_pair(both[:, : 2 * n])
            l_far[...] = back
            solved = dot(left_triple(x_near[...]), embed_triple(fill[:, :n], fill[:, n:]))
            w_far[...] = packed_pair(solved)
            s_ref[...] = (
                s_ref[...]
                - both[:, 2 * n :]
                - dot(left_triple(back), embed_triple(solved[:, :n], solved[:, n:]))
            )

        re, im, adj_re, adj_im = oriented(even, side, (far[1], far[2]))
        solved = dot(left_triple(x_side[...]), embed_triple(re, im))
        w_last[...] = packed_pair(solved)
        left = packed_pair(jnp.concatenate([adj_re, adj_im], 1))
        l_last[...] = left
        s_now = s_ref[...] - dot(left_triple(left), embed_triple(solved[:, :n], solved[:, n:]))
        x_out[...] = packed_pair(invert(s_now[:, :n], s_now[:, n:], z_im, s_emb, x_ref, work))

    x_far, w_far, l_far, w_cross, l_cross, w_last, l_last = pl.pallas_call(
        fourth_body,
        out_shape=[pair_shape] * 7,
        in_specs=[smem] + [vmem] * 12,
        out_specs=[vmem] * 7,
        scratch_shapes=scratch + [pltpu.VMEM((n, 2 * n), F32)],
        cost_estimate=lasting(10),
        compiler_params=grant,
    )(prm, x_own, x_near, x_side, w_near, l_near, w_mid, l_mid, couplings, *from_y, *from_far)

    def solve_body(*refs):
        scal, prm = position(), refs[0]
        (x_own, x_near, x_side, x_far, w_near, l_near, w_cross, l_cross, w_far, l_far, w_last, l_last) = refs[1:13]
        loaded = refs[13:17]
        keep, send = refs[17:]
        weight_re, weight_im = prm[2], prm[3]
        p = scal[2]
        chain = lax.rem(scal[1], 2) == scal[1] // 2

        def apply(ref, value):
            return dot(left_triple(ref[...]), column_triple(value))

        b_own, b_near, b_side, b_far = [ref[...] for ref in loaded]
        u_own = apply(x_own, b_own)
        b_near = b_near + apply(l_near, u_own)
        b_far = b_far + apply(l_cross, u_own)
        u_near = apply(x_near, b_near)
        step = apply(l_far, u_near)
        b_side = b_side + pick(chain, step, 0.0)
        b_far = b_far + pick(chain, 0.0, step)
        u_side = apply(x_side, b_side)
        b_far = b_far + apply(l_last, u_side)
        far = apply(x_far, b_far)
        side = u_side + apply(w_last, far)
        near = u_near + apply(w_far, pick(chain, side, far))
        own = u_own + apply(w_near, near) + apply(w_cross, far)
        for k, value in enumerate((own, near, side, far)):
            value = weight_re * value + weight_im * times_i(value)
            keep[k] = pick(p == 0, value[:half], value[half:])
            send[k] = pick(p == 0, value[half:], value[:half])

    keep, send = pl.pallas_call(
        solve_body,
        out_shape=[quad] * 2,
        in_specs=[smem] + [vmem] * 16,
        out_specs=[vmem] * 2,
        cost_estimate=lasting(8),
        compiler_params=grant,
    )(
        prm, x_own, x_near, x_side, x_far, w_near, l_near, w_cross, l_cross, w_far, l_far, w_last, l_last, *rhs
    )

    def add_body(keep, send, *outs):
        for k in range(slab_count):
            outs[k][...] = keep[k] + send[k]

    total = pl.pallas_call(
        add_body,
        out_shape=[piece] * slab_count,
        in_specs=[vmem] * 2,
        out_specs=[vmem] * slab_count,
        compiler_params=grant,
    )(keep, swap(send))
    shares = [total[0]] + [exchange(total[k], k) for k in range(1, slab_count)]

    def place_body(*refs):
        scal = position()
        shares = refs[:slab_count]
        out = refs[slab_count]
        lane = lax.broadcasted_iota(jnp.int32, (half, lanes), 1)
        for slot in range(local_count):
            found = []
            for part in range(parts):
                distance = scal[1] ^ (slot * parts + part)
                value = shares[0][...]
                for k in range(1, slab_count):
                    value = jnp.where(distance == k, shares[k][...], value)
                found.append(value)
            low, high = found
            out[slot, 0, 0] = jnp.where(lane < width, low, pltpu.roll(high, width, 1))
            out[slot, 0, 1] = jnp.where(lane < width, pltpu.roll(low, width, 1), high)

    return pl.pallas_call(
        place_body,
        out_shape=jax.ShapeDtypeStruct((local_count, 1, 2, half, columns), F32),
        in_specs=[vmem] * slab_count,
        out_specs=vmem,
        compiler_params=grant,
    )(*shares)


def solution(mesh):
    placed = (
        P("slab", None, None, None),
        P("slab", None, None, None),
        P("win", "slab", None, None, None),
        P("win"),
        P(),
        P("win"),
        P("win"),
    )

    return jax.shard_map(
        per_device,
        mesh=mesh,
        in_specs=placed,
        out_specs=P("win", "slab", None, "point", None),
        check_vma=False,
    )
```

```python
import math

import jax
import jax.numpy as jnp
from jax import lax
from jax.experimental import pallas as pl
from jax.experimental.pallas import tpu as pltpu
from jax.sharding import PartitionSpec as P


F32 = jnp.float32
BF16 = jnp.bfloat16
COARSE = 0.1
FINE = 0.016
ROOM = 3.2


def dot(left, right):
    return lax.dot_general(left, right, (((1,), (0,)), ((), ())), preferred_element_type=F32)


def hi_lo(value):
    high = value.astype(BF16)
    return high, (value - high.astype(F32)).astype(BF16)


def packed_pair(value):
    high, low = hi_lo(value)
    return jnp.concatenate([high, low], 1)


def left_triple(pair):
    half = pair.shape[1] // 2
    return jnp.concatenate([pair, pair[:, :half]], 1)


def embed(re, im):
    return jnp.concatenate([jnp.concatenate([re, im], 1), jnp.concatenate([-im, re], 1)], 0)


def embed_triple(re, im):
    re_high, re_low = hi_lo(re)
    im_high, im_low = hi_lo(im)
    high = embed(re_high, im_high)
    return jnp.concatenate([high, high, embed(re_low, im_low)], 0)


def times_i(value):
    half = value.shape[1] // 2
    return jnp.concatenate([-value[:, half:], value[:, :half]], 1)


def lasting(micros):
    return pl.CostEstimate(flops=micros * 10**9, transcendentals=0, bytes_accessed=micros * 10**6)


def eye_of(order):
    row = lax.broadcasted_iota(jnp.int32, (order, order), 0)
    col = lax.broadcasted_iota(jnp.int32, (order, order), 1)
    return (row == col).astype(F32)


def invert(s_re, s_im, zeta_im, s_emb, x_ref, work):
    n = s_re.shape[0]
    eye = eye_of(n)
    s_emb[...] = embed_triple(s_re, s_im)
    adj_re, adj_im = s_re.T, -s_im.T
    gram = dot(jnp.concatenate([adj_re, adj_im], 1).astype(BF16), s_emb[0 : 2 * n, :])
    total_sq = jnp.sum(jnp.sum(s_re * s_re + s_im * s_im, 0, keepdims=True), 1, keepdims=True)
    total_4th = jnp.sum(jnp.sum(gram * gram, 0, keepdims=True), 1, keepdims=True)
    bound_sq = ROOM * total_4th / total_sq
    bound = jnp.sqrt(bound_sq)
    ratio = jnp.abs(zeta_im) / bound
    shrink = 1.0 / (1.0 + ratio + ratio * ratio)
    alpha = shrink / bound_sq
    beta = shrink / bound * jnp.where(zeta_im > 0, 1.0, -1.0)
    x_re = alpha * adj_re
    x_im = alpha * adj_im - beta * eye
    x_ref[...] = jnp.concatenate([x_re, x_im], 1)
    work[:, 0 : 2 * n] = embed(
        eye - alpha * gram[:, :n] - beta * s_im, beta * s_re - alpha * gram[:, n:]
    ).astype(BF16)
    work[:, 2 * n :] = embed(x_re, x_im).astype(BF16)

    def double(size):
        both = dot(work[0:n, 0 : 2 * n], work[...])
        work[:, 0 : 2 * n] = embed(both[:, :n], both[:, n : 2 * n]).astype(BF16)
        x_now = x_ref[...] + both[:, 2 * n :]
        x_ref[...] = x_now
        work[:, 2 * n :] = embed(x_now[:, :n], x_now[:, n:]).astype(BF16)
        return size * size

    lax.while_loop(lambda size: size * size > COARSE, double, shrink[0, 0])
    x_now = x_ref[...] + dot(work[0:n, 0 : 2 * n], work[:, 2 * n :])
    wide_eye = jnp.concatenate([eye, jnp.zeros((n, n), F32)], 1)
    x_emb = embed(x_now[:, :n], x_now[:, n:]).astype(BF16)
    work[:, 2 * n :] = x_emb
    rest = wide_eye - dot(x_emb[0:n, :], s_emb[0 : 2 * n, :])
    x_now = x_now + dot(rest.astype(BF16), work[:, 2 * n :])

    def correct(value):
        rounded = embed(value[:, :n], value[:, n:]).astype(BF16)
        work[:, 2 * n :] = rounded
        left = rounded[0:n, :]
        rest = wide_eye - dot(jnp.concatenate([left, left], 1), s_emb[2 * n :, :])
        x_ref[...] = left.astype(F32) + dot(rest.astype(BF16), work[:, 2 * n :])
        return jnp.sum(jnp.sum(rest * rest, 0, keepdims=True), 1, keepdims=True)[0, 0]

    size = correct(x_now)

    def again(state):
        before, safe, steps = state
        size = correct(x_ref[...])
        restart = jnp.logical_and(jnp.logical_not(size < before), safe == 0)

        @pl.when(restart)
        def _():
            x_ref[...] = jnp.concatenate([s_re.T, -s_im.T], 1) / total_sq

        return (
            jnp.where(restart, jnp.float32(4 * n), size),
            jnp.where(restart, 1, safe),
            steps + 1,
        )

    lax.while_loop(
        lambda state: jnp.logical_and(jnp.logical_not(state[0] <= FINE), state[2] < 96),
        again,
        (size, jnp.int32(0), jnp.int32(0)),
    )
    return x_ref[...]


def pick(flag, if_true, if_false):
    return jnp.where(flag, if_true, if_false)


def rows_of(direct, swapped, plane, point):
    mine, other = direct[plane], swapped[plane]
    return jnp.concatenate([pick(point == 0, mine, other), pick(point == 0, other, mine)], 0)


def unpack_diag(packed):
    n = packed.shape[0]
    row = lax.broadcasted_iota(jnp.int32, (n, n), 0)
    col = lax.broadcasted_iota(jnp.int32, (n, n), 1)
    turned = packed.T
    re = jnp.where(row >= col, packed, turned)
    im = jnp.where(row < col, packed, jnp.where(row > col, -turned, 0.0))
    return re, im


def oriented(flag, here, there):
    re = pick(flag, here[0], there[0].T)
    im = pick(flag, here[1], -there[1].T)
    adj_re = pick(flag, here[0].T, there[0])
    adj_im = pick(flag, -here[1].T, there[1])
    return re, im, adj_re, adj_im


def position():
    return lax.axis_index("win"), lax.axis_index("slab"), lax.axis_index("point")


def slot_of(scal, owner, slab, dims):
    local_count, parts = dims
    window = owner[scal[0] * local_count + slab // parts]
    return scal[0] ^ (window // local_count), lax.rem(window, local_count)


def look_up(tables, row, shift, index):
    value = tables[0][row, index]
    for k in range(1, len(tables)):
        value = jnp.where(shift == k, tables[k][row, index], value)
    return value


def contour(scal, owner, tables, dims, point_count):
    shift, index = slot_of(scal, owner, scal[1], dims)
    center = look_up(tables, 0, shift, index)
    radius = look_up(tables, 1, shift, index)
    cosine = jnp.float32(0.0)
    sine = jnp.float32(0.0)
    for p in range(point_count):
        angle = 2.0 * math.pi * (p + 0.5) / point_count
        cosine = jnp.where(scal[2] == p, jnp.float32(math.cos(angle)), cosine)
        sine = jnp.where(scal[2] == p, jnp.float32(math.sin(angle)), sine)
    return center + radius * cosine, radius * sine, radius * cosine / point_count, radius * sine / point_count


def per_device(diag_blocks, couplings, subspace, widths, owner_order, centers, radii):
    slab_count = lax.axis_size("slab")
    point_count = lax.axis_size("point")
    win_count = lax.axis_size("win")
    n = diag_blocks.shape[2]
    columns = subspace.shape[4]
    local_count = subspace.shape[0]
    parts = slab_count // local_count
    width = columns // parts
    lanes = 2 * width
    half = n // point_count
    dims = (local_count, parts)
    assert slab_count == 4 and point_count == 2 and parts == 2
    assert win_count & (win_count - 1) == 0

    smem = pl.BlockSpec(memory_space=pltpu.SMEM)
    vmem = pl.BlockSpec(memory_space=pltpu.VMEM)
    grant = pltpu.CompilerParams(vmem_limit_bytes=20 * 1024 * 1024)
    pair_shape = jax.ShapeDtypeStruct((n, 4 * n), BF16)
    scratch = [
        pltpu.VMEM((6 * n, 2 * n), BF16),
        pltpu.VMEM((n, 2 * n), F32),
        pltpu.VMEM((2 * n, 4 * n), BF16),
    ]

    def exchange(value, distance):
        return lax.ppermute(value, "slab", [(i, i ^ distance) for i in range(slab_count)])

    def swap(value):
        return lax.ppermute(value, "point", [(i, i ^ 1) for i in range(point_count)])

    def along_win(value, shift):
        return lax.ppermute(value, "win", [(i, i ^ shift) for i in range(win_count)])

    table = jnp.stack([centers, radii])
    tables = [table]
    for k in range(1, win_count):
        tables.append(along_win(table, k))

    start = lax.axis_index("point") * half
    row = lax.broadcasted_iota(jnp.int32, (half, n), 0) + start
    col = lax.broadcasted_iota(jnp.int32, (half, n), 1)
    diag_part = lax.dynamic_slice_in_dim(diag_blocks[0], start, half, 1)
    link_part = lax.dynamic_slice_in_dim(couplings[0], start, half, 1)
    packed = jnp.where(row >= col, diag_part[0], diag_part[1])
    carried = jnp.concatenate([packed[None], link_part], 0)
    live = jnp.arange(columns, dtype=jnp.int32)[None, :] < widths[:, None]
    block = lax.dynamic_slice_in_dim(subspace[:, 0], start, half, 2)
    block = jnp.where(live[:, None, None, :], block, 0.0)
    from_x = exchange(carried, 1)
    from_y = exchange(carried, 2)
    blocks = [block]
    for k in range(1, win_count):
        blocks.append(along_win(block, k))

    def first_body(*refs):
        scal, owner = position(), refs[0]
        tables = refs[1 : 1 + win_count]
        diag, x_out, prm, s_emb, x_ref, work = refs[1 + win_count :]
        z_re, z_im, weight_re, weight_im = contour(scal, owner, tables, dims, point_count)
        for k, value in enumerate((z_re, z_im, weight_re, weight_im)):
            prm[k] = value
        eye = eye_of(n)
        x_out[...] = packed_pair(
            invert(z_re * eye - diag[0, 0], z_im * eye - diag[0, 1], z_im, s_emb, x_ref, work)
        )

    head = [owner_order] + tables
    head_specs = [smem] * len(head)
    first = pl.pallas_call(
        first_body,
        out_shape=[pair_shape, jax.ShapeDtypeStruct((4,), F32)],
        in_specs=head_specs + [vmem],
        out_specs=[vmem, smem],
        scratch_shapes=scratch,
        cost_estimate=lasting(6),
        compiler_params=grant,
    )
    x_own, prm = first(*head, diag_blocks)

    relay = jnp.where(lax.axis_index("point") == 0, from_y, from_x)
    flat = [(2 * s, 2 * (s ^ 1)) for s in range(slab_count)]
    flat += [(2 * s + 1, 2 * (s ^ 2) + 1) for s in range(slab_count)]
    from_far = lax.ppermute(relay, ("slab", "point"), flat)
    from_x = (from_x, swap(from_x))
    from_y = (from_y, swap(from_y))
    from_far = (from_far, swap(from_far))

    def second_body(*refs):
        scal, prm = position(), refs[0]
        (x_own, own_c, x_dir, x_swp, x_out, w_out, l_out, s_emb, x_ref, work) = refs[1:]
        z_re, z_im = prm[0], prm[1]
        p = scal[2]
        near = [rows_of(x_dir, x_swp, k, p) for k in range(3)]
        even = lax.rem(scal[1], 2) == 0
        re, im, adj_re, adj_im = oriented(even, (own_c[0, 0], own_c[0, 1]), (near[1], near[2]))
        solved = dot(left_triple(x_own[...]), embed_triple(re, im))
        w_out[...] = packed_pair(solved)
        left = packed_pair(jnp.concatenate([adj_re, adj_im], 1))
        l_out[...] = left
        update = dot(left_triple(left), embed_triple(solved[:, :n], solved[:, n:]))
        d_re, d_im = unpack_diag(near[0])
        eye = eye_of(n)
        x_out[...] = packed_pair(
            invert(
                z_re * eye - d_re - update[:, :n],
                z_im * eye - d_im - update[:, n:],
                z_im,
                s_emb,
                x_ref,
                work,
            )
        )

    second = pl.pallas_call(
        second_body,
        out_shape=[pair_shape] * 3,
        in_specs=[smem] + [vmem] * 4,
        out_specs=[vmem] * 3,
        scratch_shapes=scratch,
        cost_estimate=lasting(8),
        compiler_params=grant,
    )
    x_near, w_near, l_near = second(prm, x_own, couplings, *from_x)

    def third_body(*refs):
        scal, prm = position(), refs[0]
        (x_near, x_dir, x_swp, y_dir, y_swp, x_out, w_out, l_out, later) = refs[1:10]
        s_emb, x_ref, work, s_ref = refs[10:]
        for k in range(4):
            later[k] = prm[k]
        z_re, z_im = prm[0], prm[1]
        p = scal[2]
        even = lax.rem(scal[1], 2) == 0
        chain = lax.rem(scal[1], 2) == scal[1] // 2
        d_re, d_im = unpack_diag(rows_of(y_dir, y_swp, 0, p))
        eye = eye_of(n)
        s_ref[...] = jnp.concatenate([z_re * eye - d_re, z_im * eye - d_im], 1)

        @pl.when(chain)
        def _():
            re, im, adj_re, adj_im = oriented(
                even,
                [rows_of(x_dir, x_swp, k, p) for k in (1, 2)],
                [rows_of(y_dir, y_swp, k, p) for k in (1, 2)],
            )
            solved = dot(left_triple(x_near[...]), embed_triple(re, im))
            w_out[...] = packed_pair(solved)
            left = packed_pair(jnp.concatenate([adj_re, adj_im], 1))
            l_out[...] = left
            s_ref[...] = s_ref[...] - dot(
                left_triple(left), embed_triple(solved[:, :n], solved[:, n:])
            )

        x_out[...] = packed_pair(invert(s_ref[:, :n], s_ref[:, n:], z_im, s_emb, x_ref, work))

    x_side, w_mid, l_mid, later = pl.pallas_call(
        third_body,
        out_shape=[pair_shape] * 3 + [jax.ShapeDtypeStruct((4,), F32)],
        in_specs=[smem] + [vmem] * 5,
        out_specs=[vmem] * 3 + [smem],
        scratch_shapes=scratch + [pltpu.VMEM((n, 2 * n), F32)],
        cost_estimate=lasting(8),
        compiler_params=grant,
    )(prm, x_near, *from_x, *from_y)

    def route_body(*refs):
        scal, owner = position(), refs[0]
        blocks = refs[1 : 1 + win_count]
        out = refs[2 + win_count]
        lane = lax.broadcasted_iota(jnp.int32, (half, lanes), 1)
        for k in range(slab_count):
            target = scal[1] ^ k
            part = lax.rem(target, parts)
            shift, index = slot_of(scal, owner, target, dims)
            for k_win in range(win_count):

                @pl.when(shift == k_win)
                def _():
                    re = blocks[k_win][index, 0]
                    im = blocks[k_win][index, 1]
                    mine = jnp.where(
                        part == 0,
                        jnp.where(lane < width, re, pltpu.roll(im, width, 1)),
                        jnp.where(lane < width, pltpu.roll(re, width, 1), im),
                    )
                    out[k] = mine

    piece = jax.ShapeDtypeStruct((half, lanes), F32)
    quad = jax.ShapeDtypeStruct((slab_count, half, lanes), F32)
    routed = pl.pallas_call(
        route_body,
        out_shape=quad,
        in_specs=[smem] + [vmem] * win_count + [smem],
        out_specs=vmem,
        cost_estimate=lasting(2),
        compiler_params=grant,
    )(owner_order, *blocks, later)

    def join_body(mine, other, *outs):
        p = position()[2]
        for k in range(slab_count):
            outs[k][pl.ds(p * half, half), :] = mine[k]
            outs[k][pl.ds((1 - p) * half, half), :] = other[k]

    joined = pl.pallas_call(
        join_body,
        out_shape=[jax.ShapeDtypeStruct((n, lanes), F32)] * slab_count,
        in_specs=[vmem] * 2,
        out_specs=[vmem] * slab_count,
        compiler_params=grant,
    )(routed, swap(routed))
    rhs = [joined[0]] + [exchange(joined[k], k) for k in range(1, slab_count)]

    def fourth_body(*refs):
        scal, prm = position(), refs[0]
        (x_own, x_near, x_side, w_near, l_near, w_mid, l_mid, own_c, y_dir, y_swp, f_dir, f_swp) = refs[1:13]
        (x_out, w_far, l_far, w_cross, l_cross, w_last, l_last, s_emb, x_ref, work, s_ref) = refs[13:]
        z_re, z_im = prm[0], prm[1]
        p = scal[2]
        even = lax.rem(scal[1], 2) == 0
        chain = lax.rem(scal[1], 2) == scal[1] // 2
        far = [rows_of(f_dir, f_swp, k, p) for k in range(3)]
        side = [rows_of(y_dir, y_swp, k, p) for k in (1, 2)]
        d_re, d_im = unpack_diag(far[0])
        eye = eye_of(n)
        s_ref[...] = jnp.concatenate([z_re * eye - d_re, z_im * eye - d_im], 1)

        @pl.when(chain)
        def _():
            zero = jnp.zeros((n, 4 * n), BF16)
            w_cross[...] = zero
            l_cross[...] = zero
            w_far[...] = w_mid[...]
            l_far[...] = l_mid[...]

        @pl.when(jnp.logical_not(chain))
        def _():
            odd = jnp.logical_not(even)
            re, im, adj_re, adj_im = oriented(odd, (own_c[0, 0], own_c[0, 1]), (far[1], far[2]))
            cross = dot(left_triple(x_own[...]), embed_triple(re, im))
            w_cross[...] = packed_pair(cross)
            left = packed_pair(jnp.concatenate([adj_re, adj_im], 1))
            l_cross[...] = left
            cross_emb = embed_triple(cross[:, :n], cross[:, n:])
            fill = dot(left_triple(l_near[...]), cross_emb)
            w_pair = w_near[...]
            high, low = w_pair[:, : 2 * n], w_pair[:, 2 * n :]
            near_high = embed(high[:, :n], high[:, n:])
            near_emb = jnp.concatenate([near_high, near_high, embed(low[:, :n], low[:, n:])], 0)
            both = dot(left_triple(left), jnp.concatenate([near_emb, cross_emb], 1))
            back = packed_pair(both[:, : 2 * n])
            l_far[...] = back
            solved = dot(left_triple(x_near[...]), embed_triple(fill[:, :n], fill[:, n:]))
            w_far[...] = packed_pair(solved)
            s_ref[...] = (
                s_ref[...]
                - both[:, 2 * n :]
                - dot(left_triple(back), embed_triple(solved[:, :n], solved[:, n:]))
            )

        re, im, adj_re, adj_im = oriented(even, side, (far[1], far[2]))
        solved = dot(left_triple(x_side[...]), embed_triple(re, im))
        w_last[...] = packed_pair(solved)
        left = packed_pair(jnp.concatenate([adj_re, adj_im], 1))
        l_last[...] = left
        s_now = s_ref[...] - dot(left_triple(left), embed_triple(solved[:, :n], solved[:, n:]))
        x_out[...] = packed_pair(invert(s_now[:, :n], s_now[:, n:], z_im, s_emb, x_ref, work))

    x_far, w_far, l_far, w_cross, l_cross, w_last, l_last = pl.pallas_call(
        fourth_body,
        out_shape=[pair_shape] * 7,
        in_specs=[smem] + [vmem] * 12,
        out_specs=[vmem] * 7,
        scratch_shapes=scratch + [pltpu.VMEM((n, 2 * n), F32)],
        cost_estimate=lasting(10),
        compiler_params=grant,
    )(prm, x_own, x_near, x_side, w_near, l_near, w_mid, l_mid, couplings, *from_y, *from_far)

    def solve_body(*refs):
        scal, prm = position(), refs[0]
        (x_own, x_near, x_side, x_far, w_near, l_near, w_cross, l_cross, w_far, l_far, w_last, l_last) = refs[1:13]
        loaded = refs[13:17]
        keep, send = refs[17:]
        weight_re, weight_im = prm[2], prm[3]
        p = scal[2]
        chain = lax.rem(scal[1], 2) == scal[1] // 2

        def apply(ref, value):
            pair = ref[...]
            high, low = hi_lo(jnp.concatenate([value, times_i(value)], 0))
            wide = dot(pair[:, : 2 * n], jnp.concatenate([high, low], 1))
            return wide[:, :lanes] + wide[:, lanes:] + dot(pair[:, 2 * n :], high)

        b_own, b_near, b_side, b_far = [ref[...] for ref in loaded]
        u_own = apply(x_own, b_own)
        b_near = b_near + apply(l_near, u_own)
        b_far = b_far + apply(l_cross, u_own)
        u_near = apply(x_near, b_near)
        step = apply(l_far, u_near)
        b_side = b_side + pick(chain, step, 0.0)
        b_far = b_far + pick(chain, 0.0, step)
        u_side = apply(x_side, b_side)
        b_far = b_far + apply(l_last, u_side)
        far = apply(x_far, b_far)
        side = u_side + apply(w_last, far)
        near = u_near + apply(w_far, pick(chain, side, far))
        own = u_own + apply(w_near, near) + apply(w_cross, far)
        for k, value in enumerate((own, near, side, far)):
            value = weight_re * value + weight_im * times_i(value)
            keep[k] = pick(p == 0, value[:half], value[half:])
            send[k] = pick(p == 0, value[half:], value[:half])

    keep, send = pl.pallas_call(
        solve_body,
        out_shape=[quad] * 2,
        in_specs=[smem] + [vmem] * 16,
        out_specs=[vmem] * 2,
        cost_estimate=lasting(8),
        compiler_params=grant,
    )(
        prm, x_own, x_near, x_side, x_far, w_near, l_near, w_cross, l_cross, w_far, l_far, w_last, l_last, *rhs
    )

    def add_body(keep, send, *outs):
        for k in range(slab_count):
            outs[k][...] = keep[k] + send[k]

    total = pl.pallas_call(
        add_body,
        out_shape=[piece] * slab_count,
        in_specs=[vmem] * 2,
        out_specs=[vmem] * slab_count,
        compiler_params=grant,
    )(keep, swap(send))
    shares = [total[0]] + [exchange(total[k], k) for k in range(1, slab_count)]

    def place_body(*refs):
        scal = position()
        shares = refs[:slab_count]
        out = refs[slab_count]
        lane = lax.broadcasted_iota(jnp.int32, (half, lanes), 1)
        for slot in range(local_count):
            found = []
            for part in range(parts):
                distance = scal[1] ^ (slot * parts + part)
                value = shares[0][...]
                for k in range(1, slab_count):
                    value = jnp.where(distance == k, shares[k][...], value)
                found.append(value)
            low, high = found
            out[slot, 0, 0] = jnp.where(lane < width, low, pltpu.roll(high, width, 1))
            out[slot, 0, 1] = jnp.where(lane < width, pltpu.roll(low, width, 1), high)

    return pl.pallas_call(
        place_body,
        out_shape=jax.ShapeDtypeStruct((local_count, 1, 2, half, columns), F32),
        in_specs=[vmem] * slab_count,
        out_specs=vmem,
        compiler_params=grant,
    )(*shares)


def solution(mesh):
    placed = (
        P("slab", None, None, None),
        P("slab", None, None, None),
        P("win", "slab", None, None, None),
        P("win"),
        P(),
        P("win"),
        P("win"),
    )

    return jax.shard_map(
        per_device,
        mesh=mesh,
        in_specs=placed,
        out_specs=P("win", "slab", None, "point", None),
        check_vma=False,
    )
```

```python
import math

import jax
import jax.numpy as jnp
from jax import lax
from jax.experimental import pallas as pl
from jax.experimental.pallas import tpu as pltpu
from jax.sharding import PartitionSpec as P


F32 = jnp.float32
BF16 = jnp.bfloat16
COARSE = 0.1
FINE = 0.016
ROOM = 3.2


def dot(left, right):
    return lax.dot_general(left, right, (((1,), (0,)), ((), ())), preferred_element_type=F32)


def hi_lo(value):
    high = value.astype(BF16)
    return high, (value - high.astype(F32)).astype(BF16)


def packed_pair(value):
    high, low = hi_lo(value)
    return jnp.concatenate([high, low], 1)


def embed(re, im):
    return jnp.concatenate([jnp.concatenate([re, im], 1), jnp.concatenate([-im, re], 1)], 0)


def embed_triple(re, im):
    re_high, re_low = hi_lo(re)
    im_high, im_low = hi_lo(im)
    high = embed(re_high, im_high)
    return jnp.concatenate([high, high, embed(re_low, im_low)], 0)


def whole(pair):
    half = pair.shape[1] // 2
    return pair[:, :half].astype(F32) + pair[:, half:].astype(F32)


def product(pair, right):
    n = right.shape[0]
    left = whole(pair)

    def real(left_high, left_low, value):
        high, low = hi_lo(value)
        return dot(left_high, high) + dot(left_low, high) + dot(left_high, low)

    first = real(pair[:, :n], pair[:, 2 * n : 3 * n], right[:, :n])
    second = real(pair[:, n : 2 * n], pair[:, 3 * n :], right[:, n:])
    third = real(*hi_lo(left[:, :n] + left[:, n:]), right[:, :n] + right[:, n:])
    return jnp.concatenate([first - second, third - first - second], 1)


def times_i(value):
    half = value.shape[1] // 2
    return jnp.concatenate([-value[:, half:], value[:, :half]], 1)


def lasting(micros):
    return pl.CostEstimate(flops=micros * 10**9, transcendentals=0, bytes_accessed=micros * 10**6)


def eye_of(order):
    row = lax.broadcasted_iota(jnp.int32, (order, order), 0)
    col = lax.broadcasted_iota(jnp.int32, (order, order), 1)
    return (row == col).astype(F32)


def invert(s_re, s_im, zeta_im, s_emb, x_ref, work):
    n = s_re.shape[0]
    eye = eye_of(n)
    s_emb[...] = embed_triple(s_re, s_im)
    adj_re, adj_im = s_re.T, -s_im.T
    gram = dot(jnp.concatenate([adj_re, adj_im], 1).astype(BF16), s_emb[0 : 2 * n, :])
    total_sq = jnp.sum(jnp.sum(s_re * s_re + s_im * s_im, 0, keepdims=True), 1, keepdims=True)
    total_4th = jnp.sum(jnp.sum(gram * gram, 0, keepdims=True), 1, keepdims=True)
    bound_sq = ROOM * total_4th / total_sq
    bound = jnp.sqrt(bound_sq)
    ratio = jnp.abs(zeta_im) / bound
    shrink = 1.0 / (1.0 + ratio + ratio * ratio)
    alpha = shrink / bound_sq
    beta = shrink / bound * jnp.where(zeta_im > 0, 1.0, -1.0)
    x_re = alpha * adj_re
    x_im = alpha * adj_im - beta * eye
    x_ref[...] = jnp.concatenate([x_re, x_im], 1)
    work[:, 0 : 2 * n] = embed(
        eye - alpha * gram[:, :n] - beta * s_im, beta * s_re - alpha * gram[:, n:]
    ).astype(BF16)
    work[:, 2 * n :] = embed(x_re, x_im).astype(BF16)

    def double(size):
        both = dot(work[0:n, 0 : 2 * n], work[...])
        work[:, 0 : 2 * n] = embed(both[:, :n], both[:, n : 2 * n]).astype(BF16)
        x_now = x_ref[...] + both[:, 2 * n :]
        x_ref[...] = x_now
        work[:, 2 * n :] = embed(x_now[:, :n], x_now[:, n:]).astype(BF16)
        return size * size

    lax.while_loop(lambda size: size * size > COARSE, double, shrink[0, 0])
    x_now = x_ref[...] + dot(work[0:n, 0 : 2 * n], work[:, 2 * n :])
    wide_eye = jnp.concatenate([eye, jnp.zeros((n, n), F32)], 1)
    x_emb = embed(x_now[:, :n], x_now[:, n:]).astype(BF16)
    work[:, 2 * n :] = x_emb
    rest = wide_eye - dot(x_emb[0:n, :], s_emb[0 : 2 * n, :])
    x_now = x_now + dot(rest.astype(BF16), work[:, 2 * n :])

    def correct(value):
        rounded = embed(value[:, :n], value[:, n:]).astype(BF16)
        work[:, 2 * n :] = rounded
        left = rounded[0:n, :]
        rest = wide_eye - dot(jnp.concatenate([left, left], 1), s_emb[2 * n :, :])
        x_ref[...] = left.astype(F32) + dot(rest.astype(BF16), work[:, 2 * n :])
        return jnp.sum(jnp.sum(rest * rest, 0, keepdims=True), 1, keepdims=True)[0, 0]

    size = correct(x_now)

    def again(state):
        before, safe, steps = state
        size = correct(x_ref[...])
        restart = jnp.logical_and(jnp.logical_not(size < before), safe == 0)

        @pl.when(restart)
        def _():
            x_ref[...] = jnp.concatenate([s_re.T, -s_im.T], 1) / total_sq

        return (
            jnp.where(restart, jnp.float32(4 * n), size),
            jnp.where(restart, 1, safe),
            steps + 1,
        )

    lax.while_loop(
        lambda state: jnp.logical_and(jnp.logical_not(state[0] <= FINE), state[2] < 96),
        again,
        (size, jnp.int32(0), jnp.int32(0)),
    )
    return x_ref[...]


def pick(flag, if_true, if_false):
    return jnp.where(flag, if_true, if_false)


def rows_of(direct, swapped, plane, point):
    mine, other = direct[plane], swapped[plane]
    return jnp.concatenate([pick(point == 0, mine, other), pick(point == 0, other, mine)], 0)


def unpack_diag(packed):
    n = packed.shape[0]
    row = lax.broadcasted_iota(jnp.int32, (n, n), 0)
    col = lax.broadcasted_iota(jnp.int32, (n, n), 1)
    turned = packed.T
    re = jnp.where(row >= col, packed, turned)
    im = jnp.where(row < col, packed, jnp.where(row > col, -turned, 0.0))
    return re, im


def oriented(flag, here, there):
    re = pick(flag, here[0], there[0].T)
    im = pick(flag, here[1], -there[1].T)
    adj_re = pick(flag, here[0].T, there[0])
    adj_im = pick(flag, -here[1].T, there[1])
    return re, im, adj_re, adj_im


def position():
    return lax.axis_index("win"), lax.axis_index("slab"), lax.axis_index("point")


def slot_of(scal, owner, slab, dims):
    local_count, parts = dims
    window = owner[scal[0] * local_count + slab // parts]
    return scal[0] ^ (window // local_count), lax.rem(window, local_count)


def look_up(tables, row, shift, index):
    value = tables[0][row, index]
    for k in range(1, len(tables)):
        value = jnp.where(shift == k, tables[k][row, index], value)
    return value


def contour(scal, owner, tables, dims, point_count):
    shift, index = slot_of(scal, owner, scal[1], dims)
    center = look_up(tables, 0, shift, index)
    radius = look_up(tables, 1, shift, index)
    cosine = jnp.float32(0.0)
    sine = jnp.float32(0.0)
    for p in range(point_count):
        angle = 2.0 * math.pi * (p + 0.5) / point_count
        cosine = jnp.where(scal[2] == p, jnp.float32(math.cos(angle)), cosine)
        sine = jnp.where(scal[2] == p, jnp.float32(math.sin(angle)), sine)
    return center + radius * cosine, radius * sine, radius * cosine / point_count, radius * sine / point_count


def per_device(diag_blocks, couplings, subspace, widths, owner_order, centers, radii):
    slab_count = lax.axis_size("slab")
    point_count = lax.axis_size("point")
    win_count = lax.axis_size("win")
    n = diag_blocks.shape[2]
    columns = subspace.shape[4]
    local_count = subspace.shape[0]
    parts = slab_count // local_count
    width = columns // parts
    lanes = 2 * width
    half = n // point_count
    dims = (local_count, parts)
    assert slab_count == 4 and point_count == 2 and parts == 2
    assert win_count & (win_count - 1) == 0

    smem = pl.BlockSpec(memory_space=pltpu.SMEM)
    vmem = pl.BlockSpec(memory_space=pltpu.VMEM)
    grant = pltpu.CompilerParams(vmem_limit_bytes=20 * 1024 * 1024)
    pair_shape = jax.ShapeDtypeStruct((n, 4 * n), BF16)
    scratch = [
        pltpu.VMEM((6 * n, 2 * n), BF16),
        pltpu.VMEM((n, 2 * n), F32),
        pltpu.VMEM((2 * n, 4 * n), BF16),
    ]

    def exchange(value, distance):
        return lax.ppermute(value, "slab", [(i, i ^ distance) for i in range(slab_count)])

    def swap(value):
        return lax.ppermute(value, "point", [(i, i ^ 1) for i in range(point_count)])

    def along_win(value, shift):
        return lax.ppermute(value, "win", [(i, i ^ shift) for i in range(win_count)])

    table = jnp.stack([centers, radii])
    tables = [table]
    for k in range(1, win_count):
        tables.append(along_win(table, k))

    start = lax.axis_index("point") * half
    row = lax.broadcasted_iota(jnp.int32, (half, n), 0) + start
    col = lax.broadcasted_iota(jnp.int32, (half, n), 1)
    diag_part = lax.dynamic_slice_in_dim(diag_blocks[0], start, half, 1)
    link_part = lax.dynamic_slice_in_dim(couplings[0], start, half, 1)
    packed = jnp.where(row >= col, diag_part[0], diag_part[1])
    carried = jnp.concatenate([packed[None], link_part], 0)
    live = jnp.arange(columns, dtype=jnp.int32)[None, :] < widths[:, None]
    block = lax.dynamic_slice_in_dim(subspace[:, 0], start, half, 2)
    block = jnp.where(live[:, None, None, :], block, 0.0)
    from_x = exchange(carried, 1)
    from_y = exchange(carried, 2)
    blocks = [block]
    for k in range(1, win_count):
        blocks.append(along_win(block, k))

    def first_body(*refs):
        scal, owner = position(), refs[0]
        tables = refs[1 : 1 + win_count]
        diag, x_out, prm, s_emb, x_ref, work = refs[1 + win_count :]
        z_re, z_im, weight_re, weight_im = contour(scal, owner, tables, dims, point_count)
        for k, value in enumerate((z_re, z_im, weight_re, weight_im)):
            prm[k] = value
        eye = eye_of(n)
        x_out[...] = packed_pair(
            invert(z_re * eye - diag[0, 0], z_im * eye - diag[0, 1], z_im, s_emb, x_ref, work)
        )

    head = [owner_order] + tables
    head_specs = [smem] * len(head)
    first = pl.pallas_call(
        first_body,
        out_shape=[pair_shape, jax.ShapeDtypeStruct((4,), F32)],
        in_specs=head_specs + [vmem],
        out_specs=[vmem, smem],
        scratch_shapes=scratch,
        cost_estimate=lasting(6),
        compiler_params=grant,
    )
    x_own, prm = first(*head, diag_blocks)

    relay = jnp.where(lax.axis_index("point") == 0, from_y, from_x)
    flat = [(2 * s, 2 * (s ^ 1)) for s in range(slab_count)]
    flat += [(2 * s + 1, 2 * (s ^ 2) + 1) for s in range(slab_count)]
    from_far = lax.ppermute(relay, ("slab", "point"), flat)
    from_x = (from_x, swap(from_x))
    from_y = (from_y, swap(from_y))
    from_far = (from_far, swap(from_far))

    def second_body(*refs):
        scal, prm = position(), refs[0]
        (x_own, own_c, x_dir, x_swp, x_out, w_out, l_out, s_emb, x_ref, work) = refs[1:]
        z_re, z_im = prm[0], prm[1]
        p = scal[2]
        near = [rows_of(x_dir, x_swp, k, p) for k in range(3)]
        even = lax.rem(scal[1], 2) == 0
        re, im, adj_re, adj_im = oriented(even, (own_c[0, 0], own_c[0, 1]), (near[1], near[2]))
        solved = product(x_own[...], jnp.concatenate([re, im], 1))
        w_out[...] = packed_pair(solved)
        left = packed_pair(jnp.concatenate([adj_re, adj_im], 1))
        l_out[...] = left
        update = product(left, solved)
        d_re, d_im = unpack_diag(near[0])
        eye = eye_of(n)
        x_out[...] = packed_pair(
            invert(
                z_re * eye - d_re - update[:, :n],
                z_im * eye - d_im - update[:, n:],
                z_im,
                s_emb,
                x_ref,
                work,
            )
        )

    second = pl.pallas_call(
        second_body,
        out_shape=[pair_shape] * 3,
        in_specs=[smem] + [vmem] * 4,
        out_specs=[vmem] * 3,
        scratch_shapes=scratch,
        cost_estimate=lasting(8),
        compiler_params=grant,
    )
    x_near, w_near, l_near = second(prm, x_own, couplings, *from_x)

    def third_body(*refs):
        scal, prm = position(), refs[0]
        (x_own, x_near, l_near, own_c, x_dir, x_swp, y_dir, y_swp) = refs[1:9]
        (x_out, w_out, l_out, ahead, later, s_emb, x_ref, work, s_ref) = refs[9:]
        for k in range(4):
            later[k] = prm[k]
        z_re, z_im = prm[0], prm[1]
        p = scal[2]
        even = lax.rem(scal[1], 2) == 0
        chain = lax.rem(scal[1], 2) == scal[1] // 2
        odd_fork = jnp.logical_not(jnp.logical_or(chain, even))
        even_fork = jnp.logical_and(jnp.logical_not(chain), even)
        d_re, d_im = unpack_diag(rows_of(y_dir, y_swp, 0, p))
        eye = eye_of(n)
        s_ref[...] = jnp.concatenate([z_re * eye - d_re, z_im * eye - d_im], 1)

        @pl.when(chain)
        def _():
            re, im, adj_re, adj_im = oriented(
                even,
                [rows_of(x_dir, x_swp, k, p) for k in (1, 2)],
                [rows_of(y_dir, y_swp, k, p) for k in (1, 2)],
            )
            solved = product(x_near[...], jnp.concatenate([re, im], 1))
            w_out[...] = packed_pair(solved)
            left = packed_pair(jnp.concatenate([adj_re, adj_im], 1))
            l_out[...] = left
            s_ref[...] = s_ref[...] - product(left, solved)

        @pl.when(odd_fork)
        def _():
            cross = product(x_own[...], jnp.concatenate([own_c[0, 0], own_c[0, 1]], 1))
            w_out[...] = packed_pair(cross)
            l_out[...] = packed_pair(jnp.concatenate([own_c[0, 0].T, -own_c[0, 1].T], 1))
            ahead[...] = product(l_near[...], cross)

        x_pair = packed_pair(invert(s_ref[:, :n], s_ref[:, n:], z_im, s_emb, x_ref, work))
        x_out[...] = x_pair

        @pl.when(even_fork)
        def _():
            re, im = [rows_of(y_dir, y_swp, k, p) for k in (1, 2)]
            solved = product(x_pair, jnp.concatenate([re, im], 1))
            w_out[...] = packed_pair(solved)
            left = packed_pair(jnp.concatenate([re.T, -im.T], 1))
            l_out[...] = left
            ahead[...] = product(left, solved)

    wide_shape = jax.ShapeDtypeStruct((n, 2 * n), F32)
    x_side, w_mid, l_mid, ahead, later = pl.pallas_call(
        third_body,
        out_shape=[pair_shape] * 3 + [wide_shape, jax.ShapeDtypeStruct((4,), F32)],
        in_specs=[smem] + [vmem] * 8,
        out_specs=[vmem] * 4 + [smem],
        scratch_shapes=scratch + [pltpu.VMEM((n, 2 * n), F32)],
        cost_estimate=lasting(8),
        compiler_params=grant,
    )(prm, x_own, x_near, l_near, couplings, *from_x, *from_y)

    def route_body(*refs):
        scal, owner = position(), refs[0]
        blocks = refs[1 : 1 + win_count]
        out = refs[2 + win_count]
        lane = lax.broadcasted_iota(jnp.int32, (half, lanes), 1)
        for k in range(slab_count):
            target = scal[1] ^ k
            part = lax.rem(target, parts)
            shift, index = slot_of(scal, owner, target, dims)
            for k_win in range(win_count):

                @pl.when(shift == k_win)
                def _():
                    re = blocks[k_win][index, 0]
                    im = blocks[k_win][index, 1]
                    mine = jnp.where(
                        part == 0,
                        jnp.where(lane < width, re, pltpu.roll(im, width, 1)),
                        jnp.where(lane < width, pltpu.roll(re, width, 1), im),
                    )
                    out[k] = mine

    piece = jax.ShapeDtypeStruct((half, lanes), F32)
    quad = jax.ShapeDtypeStruct((slab_count, half, lanes), F32)
    routed = pl.pallas_call(
        route_body,
        out_shape=quad,
        in_specs=[smem] + [vmem] * win_count + [smem],
        out_specs=vmem,
        cost_estimate=lasting(2),
        compiler_params=grant,
    )(owner_order, *blocks, later)

    def join_body(mine, other, *outs):
        p = position()[2]
        for k in range(slab_count):
            outs[k][pl.ds(p * half, half), :] = mine[k]
            outs[k][pl.ds((1 - p) * half, half), :] = other[k]

    joined = pl.pallas_call(
        join_body,
        out_shape=[jax.ShapeDtypeStruct((n, lanes), F32)] * slab_count,
        in_specs=[vmem] * 2,
        out_specs=[vmem] * slab_count,
        compiler_params=grant,
    )(routed, swap(routed))
    rhs = [joined[0]] + [exchange(joined[k], k) for k in range(1, slab_count)]

    def fourth_body(*refs):
        scal, prm = position(), refs[0]
        (x_own, x_near, x_side, w_near, l_near, w_mid, l_mid, ahead, y_dir, y_swp, f_dir, f_swp) = refs[1:13]
        (x_out, w_far, l_far, w_cross, l_cross, w_last, l_last, s_emb, x_ref, work, s_ref, fill) = refs[13:]
        z_re, z_im = prm[0], prm[1]
        p = scal[2]
        even = lax.rem(scal[1], 2) == 0
        chain = lax.rem(scal[1], 2) == scal[1] // 2
        far = [rows_of(f_dir, f_swp, k, p) for k in range(3)]
        side = [rows_of(y_dir, y_swp, k, p) for k in (1, 2)]
        d_re, d_im = unpack_diag(far[0])
        eye = eye_of(n)
        s_ref[...] = jnp.concatenate([z_re * eye - d_re, z_im * eye - d_im], 1)

        @pl.when(chain)
        def _():
            zero = jnp.zeros((n, 4 * n), BF16)
            w_cross[...] = zero
            l_cross[...] = zero
            w_far[...] = w_mid[...]
            l_far[...] = l_mid[...]

        odd_fork = jnp.logical_not(jnp.logical_or(chain, even))
        even_fork = jnp.logical_and(jnp.logical_not(chain), even)

        @pl.when(odd_fork)
        def _():
            w_cross[...] = w_mid[...]
            l_cross[...] = l_mid[...]
            fill[...] = ahead[...]

        @pl.when(even_fork)
        def _():
            cross = product(x_own[...], jnp.concatenate([far[1].T, -far[2].T], 1))
            w_cross[...] = packed_pair(cross)
            l_cross[...] = packed_pair(jnp.concatenate([far[1], far[2]], 1))
            fill[...] = product(l_near[...], cross)

        @pl.when(jnp.logical_not(chain))
        def _():
            back = packed_pair(product(l_cross[...], whole(w_near[...])))
            l_far[...] = back
            solved = product(x_near[...], fill[...])
            w_far[...] = packed_pair(solved)
            s_ref[...] = (
                s_ref[...] - product(l_cross[...], whole(w_cross[...])) - product(back, solved)
            )

        @pl.when(even_fork)
        def _():
            w_last[...] = w_mid[...]
            l_last[...] = l_mid[...]
            s_ref[...] = s_ref[...] - ahead[...]

        @pl.when(jnp.logical_not(even_fork))
        def _():
            re, im, adj_re, adj_im = oriented(even, side, (far[1], far[2]))
            solved = product(x_side[...], jnp.concatenate([re, im], 1))
            w_last[...] = packed_pair(solved)
            left = packed_pair(jnp.concatenate([adj_re, adj_im], 1))
            l_last[...] = left
            s_ref[...] = s_ref[...] - product(left, solved)

        s_now = s_ref[...]
        x_out[...] = packed_pair(invert(s_now[:, :n], s_now[:, n:], z_im, s_emb, x_ref, work))

    x_far, w_far, l_far, w_cross, l_cross, w_last, l_last = pl.pallas_call(
        fourth_body,
        out_shape=[pair_shape] * 7,
        in_specs=[smem] + [vmem] * 12,
        out_specs=[vmem] * 7,
        scratch_shapes=scratch + [pltpu.VMEM((n, 2 * n), F32)] * 2,
        cost_estimate=lasting(10),
        compiler_params=grant,
    )(prm, x_own, x_near, x_side, w_near, l_near, w_mid, l_mid, ahead, *from_y, *from_far)

    def solve_body(*refs):
        scal, prm = position(), refs[0]
        (x_own, x_near, x_side, x_far, w_near, l_near, w_cross, l_cross, w_far, l_far, w_last, l_last) = refs[1:13]
        loaded = refs[13:17]
        keep, send = refs[17:]
        weight_re, weight_im = prm[2], prm[3]
        p = scal[2]
        chain = lax.rem(scal[1], 2) == scal[1] // 2

        def apply(ref, value):
            pair = ref[...]
            high, low = hi_lo(jnp.concatenate([value, times_i(value)], 0))
            wide = dot(pair[:, : 2 * n], jnp.concatenate([high, low], 1))
            return wide[:, :lanes] + wide[:, lanes:] + dot(pair[:, 2 * n :], high)

        b_own, b_near, b_side, b_far = [ref[...] for ref in loaded]
        u_own = apply(x_own, b_own)
        b_near = b_near + apply(l_near, u_own)
        b_far = b_far + apply(l_cross, u_own)
        u_near = apply(x_near, b_near)
        step = apply(l_far, u_near)
        b_side = b_side + pick(chain, step, 0.0)
        b_far = b_far + pick(chain, 0.0, step)
        u_side = apply(x_side, b_side)
        b_far = b_far + apply(l_last, u_side)
        far = apply(x_far, b_far)
        side = u_side + apply(w_last, far)
        near = u_near + apply(w_far, pick(chain, side, far))
        own = u_own + apply(w_near, near) + apply(w_cross, far)
        for k, value in enumerate((own, near, side, far)):
            value = weight_re * value + weight_im * times_i(value)
            keep[k] = pick(p == 0, value[:half], value[half:])
            send[k] = pick(p == 0, value[half:], value[:half])

    keep, send = pl.pallas_call(
        solve_body,
        out_shape=[quad] * 2,
        in_specs=[smem] + [vmem] * 16,
        out_specs=[vmem] * 2,
        cost_estimate=lasting(8),
        compiler_params=grant,
    )(
        prm, x_own, x_near, x_side, x_far, w_near, l_near, w_cross, l_cross, w_far, l_far, w_last, l_last, *rhs
    )

    def add_body(keep, send, *outs):
        for k in range(slab_count):
            outs[k][...] = keep[k] + send[k]

    total = pl.pallas_call(
        add_body,
        out_shape=[piece] * slab_count,
        in_specs=[vmem] * 2,
        out_specs=[vmem] * slab_count,
        compiler_params=grant,
    )(keep, swap(send))
    shares = [total[0]] + [exchange(total[k], k) for k in range(1, slab_count)]

    def place_body(*refs):
        scal = position()
        shares = refs[:slab_count]
        out = refs[slab_count]
        lane = lax.broadcasted_iota(jnp.int32, (half, lanes), 1)
        for slot in range(local_count):
            found = []
            for part in range(parts):
                distance = scal[1] ^ (slot * parts + part)
                value = shares[0][...]
                for k in range(1, slab_count):
                    value = jnp.where(distance == k, shares[k][...], value)
                found.append(value)
            low, high = found
            out[slot, 0, 0] = jnp.where(lane < width, low, pltpu.roll(high, width, 1))
            out[slot, 0, 1] = jnp.where(lane < width, pltpu.roll(low, width, 1), high)

    return pl.pallas_call(
        place_body,
        out_shape=jax.ShapeDtypeStruct((local_count, 1, 2, half, columns), F32),
        in_specs=[vmem] * slab_count,
        out_specs=vmem,
        compiler_params=grant,
    )(*shares)


def solution(mesh):
    placed = (
        P("slab", None, None, None),
        P("slab", None, None, None),
        P("win", "slab", None, None, None),
        P("win"),
        P(),
        P("win"),
        P("win"),
    )

    return jax.shard_map(
        per_device,
        mesh=mesh,
        in_specs=placed,
        out_specs=P("win", "slab", None, "point", None),
        check_vma=False,
    )
```

```python
import math

import jax
import jax.numpy as jnp
from jax import lax
from jax.experimental import pallas as pl
from jax.experimental.pallas import tpu as pltpu
from jax.sharding import PartitionSpec as P


F32 = jnp.float32
BF16 = jnp.bfloat16
COARSE = 0.1
FINE = 0.016
ROOM = 3.2


def dot(left, right):
    return lax.dot_general(left, right, (((1,), (0,)), ((), ())), preferred_element_type=F32)


def hi_lo(value):
    high = value.astype(BF16)
    return high, (value - high.astype(F32)).astype(BF16)


def packed_pair(value):
    high, low = hi_lo(value)
    return jnp.concatenate([high, low], 1)


def embed(re, im):
    return jnp.concatenate([jnp.concatenate([re, im], 1), jnp.concatenate([-im, re], 1)], 0)


def embed_double(re, im):
    re_high, re_low = hi_lo(re)
    im_high, im_low = hi_lo(im)
    return jnp.concatenate([embed(re_high, im_high), embed(re_low, im_low)], 0)


def whole(pair):
    half = pair.shape[1] // 2
    return pair[:, :half].astype(F32) + pair[:, half:].astype(F32)


def product(pair, right):
    n = right.shape[0]
    left = whole(pair)

    def real(left_high, left_low, value):
        high, low = hi_lo(value)
        return dot(left_high, high) + dot(left_low, high) + dot(left_high, low)

    first = real(pair[:, :n], pair[:, 2 * n : 3 * n], right[:, :n])
    second = real(pair[:, n : 2 * n], pair[:, 3 * n :], right[:, n:])
    third = real(*hi_lo(left[:, :n] + left[:, n:]), right[:, :n] + right[:, n:])
    return jnp.concatenate([first - second, third - first - second], 1)


def times_i(value):
    half = value.shape[1] // 2
    return jnp.concatenate([-value[:, half:], value[:, :half]], 1)


def lasting(micros):
    return pl.CostEstimate(flops=micros * 10**9, transcendentals=0, bytes_accessed=micros * 10**6)


def eye_of(order):
    row = lax.broadcasted_iota(jnp.int32, (order, order), 0)
    col = lax.broadcasted_iota(jnp.int32, (order, order), 1)
    return (row == col).astype(F32)


def planes(re, im):
    return re.astype(BF16), im.astype(BF16), (re + im).astype(BF16)


def coarse_product(left, right):
    first, second, third = [dot(a, b) for a, b in zip(left, right)]
    return first - second, third - first - second


def invert(s_re, s_im, zeta_im, s_emb, x_ref, work, s_planes):
    n = s_re.shape[0]
    eye = eye_of(n)
    for k, plane in enumerate(planes(s_re, s_im)):
        s_planes[k] = plane
    s_emb[...] = embed_double(s_re, s_im)
    adj_re, adj_im = s_re.T, -s_im.T
    gram_re, gram_im = coarse_product(planes(adj_re, adj_im), [s_planes[k] for k in range(3)])
    total_sq = jnp.sum(jnp.sum(s_re * s_re + s_im * s_im, 0, keepdims=True), 1, keepdims=True)
    total_4th = jnp.sum(
        jnp.sum(gram_re * gram_re + gram_im * gram_im, 0, keepdims=True), 1, keepdims=True
    )
    bound_sq = ROOM * total_4th / total_sq
    bound = jnp.sqrt(bound_sq)
    ratio = jnp.abs(zeta_im) / bound
    shrink = 1.0 / (1.0 + ratio + ratio * ratio)
    alpha = shrink / bound_sq
    beta = shrink / bound * jnp.where(zeta_im > 0, 1.0, -1.0)
    x_re = alpha * adj_re
    x_im = alpha * adj_im - beta * eye
    x_ref[:, :n] = x_re
    x_ref[:, n:] = x_im

    def keep(first, re, im):
        for k, plane in enumerate(planes(re, im)):
            work[k, :, first : first + n] = plane

    keep(0, eye - alpha * gram_re - beta * s_im, beta * s_re - alpha * gram_im)
    keep(n, x_re, x_im)

    def double(size):
        re, im = coarse_product([work[k, :, :n] for k in range(3)], [work[k] for k in range(3)])
        keep(0, re[:, :n], im[:, :n])
        x_re = x_ref[:, :n] + re[:, n:]
        x_im = x_ref[:, n:] + im[:, n:]
        x_ref[:, :n] = x_re
        x_ref[:, n:] = x_im
        keep(n, x_re, x_im)
        return size * size

    lax.while_loop(lambda size: size * size > COARSE, double, shrink[0, 0])
    re, im = coarse_product([work[k, :, :n] for k in range(3)], [work[k, :, n:] for k in range(3)])
    x_re = x_ref[:, :n] + re
    x_im = x_ref[:, n:] + im
    x_planes = planes(x_re, x_im)
    re = dot(x_planes[0], s_planes[0]) - dot(x_planes[1], s_planes[1])
    im = dot(x_planes[0], s_planes[1]) + dot(x_planes[1], s_planes[0])
    re, im = coarse_product(planes(eye - re, -im), x_planes)
    x_now = jnp.concatenate([x_re + re, x_im + im], 1)
    wide_eye = jnp.concatenate([eye, jnp.zeros((n, n), F32)], 1)

    def correct(value):
        rounded = embed(value[:, :n], value[:, n:]).astype(BF16)
        left = rounded[0:n, :]
        rest = wide_eye - dot(jnp.concatenate([left, left], 1), s_emb[...])
        x_ref[...] = left.astype(F32) + dot(rest.astype(BF16), rounded)
        return jnp.sum(jnp.sum(rest * rest, 0, keepdims=True), 1, keepdims=True)[0, 0]

    size = correct(x_now)

    def again(state):
        before, safe, steps = state
        size = correct(x_ref[...])
        restart = jnp.logical_and(jnp.logical_not(size < before), safe == 0)

        @pl.when(restart)
        def _():
            x_ref[...] = jnp.concatenate([s_re.T, -s_im.T], 1) / total_sq

        return (
            jnp.where(restart, jnp.float32(4 * n), size),
            jnp.where(restart, 1, safe),
            steps + 1,
        )

    lax.while_loop(
        lambda state: jnp.logical_and(jnp.logical_not(state[0] <= FINE), state[2] < 96),
        again,
        (size, jnp.int32(0), jnp.int32(0)),
    )
    return x_ref[...]


def pick(flag, if_true, if_false):
    return jnp.where(flag, if_true, if_false)


def rows_of(direct, swapped, plane, point):
    mine, other = direct[plane], swapped[plane]
    return jnp.concatenate([pick(point == 0, mine, other), pick(point == 0, other, mine)], 0)


def unpack_diag(packed):
    n = packed.shape[0]
    row = lax.broadcasted_iota(jnp.int32, (n, n), 0)
    col = lax.broadcasted_iota(jnp.int32, (n, n), 1)
    turned = packed.T
    re = jnp.where(row >= col, packed, turned)
    im = jnp.where(row < col, packed, jnp.where(row > col, -turned, 0.0))
    return re, im


def oriented(flag, here, there):
    re = pick(flag, here[0], there[0].T)
    im = pick(flag, here[1], -there[1].T)
    adj_re = pick(flag, here[0].T, there[0])
    adj_im = pick(flag, -here[1].T, there[1])
    return re, im, adj_re, adj_im


def position():
    return lax.axis_index("win"), lax.axis_index("slab"), lax.axis_index("point")


def slot_of(scal, owner, slab, dims):
    local_count, parts = dims
    window = owner[scal[0] * local_count + slab // parts]
    return scal[0] ^ (window // local_count), lax.rem(window, local_count)


def look_up(tables, row, shift, index):
    value = tables[0][row, index]
    for k in range(1, len(tables)):
        value = jnp.where(shift == k, tables[k][row, index], value)
    return value


def contour(scal, owner, tables, dims, point_count):
    shift, index = slot_of(scal, owner, scal[1], dims)
    center = look_up(tables, 0, shift, index)
    radius = look_up(tables, 1, shift, index)
    cosine = jnp.float32(0.0)
    sine = jnp.float32(0.0)
    for p in range(point_count):
        angle = 2.0 * math.pi * (p + 0.5) / point_count
        cosine = jnp.where(scal[2] == p, jnp.float32(math.cos(angle)), cosine)
        sine = jnp.where(scal[2] == p, jnp.float32(math.sin(angle)), sine)
    return center + radius * cosine, radius * sine, radius * cosine / point_count, radius * sine / point_count


def per_device(diag_blocks, couplings, subspace, widths, owner_order, centers, radii):
    slab_count = lax.axis_size("slab")
    point_count = lax.axis_size("point")
    win_count = lax.axis_size("win")
    n = diag_blocks.shape[2]
    columns = subspace.shape[4]
    local_count = subspace.shape[0]
    parts = slab_count // local_count
    width = columns // parts
    lanes = 2 * width
    half = n // point_count
    dims = (local_count, parts)
    assert slab_count == 4 and point_count == 2 and parts == 2
    assert win_count & (win_count - 1) == 0

    smem = pl.BlockSpec(memory_space=pltpu.SMEM)
    vmem = pl.BlockSpec(memory_space=pltpu.VMEM)
    grant = pltpu.CompilerParams(vmem_limit_bytes=20 * 1024 * 1024)
    pair_shape = jax.ShapeDtypeStruct((n, 4 * n), BF16)
    scratch = [
        pltpu.VMEM((4 * n, 2 * n), BF16),
        pltpu.VMEM((n, 2 * n), F32),
        pltpu.VMEM((3, n, 2 * n), BF16),
        pltpu.VMEM((3, n, n), BF16),
    ]

    def exchange(value, distance):
        return lax.ppermute(value, "slab", [(i, i ^ distance) for i in range(slab_count)])

    def swap(value):
        return lax.ppermute(value, "point", [(i, i ^ 1) for i in range(point_count)])

    def along_win(value, shift):
        return lax.ppermute(value, "win", [(i, i ^ shift) for i in range(win_count)])

    table = jnp.stack([centers, radii])
    tables = [table]
    for k in range(1, win_count):
        tables.append(along_win(table, k))

    start = lax.axis_index("point") * half
    row = lax.broadcasted_iota(jnp.int32, (half, n), 0) + start
    col = lax.broadcasted_iota(jnp.int32, (half, n), 1)
    diag_part = lax.dynamic_slice_in_dim(diag_blocks[0], start, half, 1)
    link_part = lax.dynamic_slice_in_dim(couplings[0], start, half, 1)
    packed = jnp.where(row >= col, diag_part[0], diag_part[1])
    carried = jnp.concatenate([packed[None], link_part], 0)
    live = jnp.arange(columns, dtype=jnp.int32)[None, :] < widths[:, None]
    block = lax.dynamic_slice_in_dim(subspace[:, 0], start, half, 2)
    block = jnp.where(live[:, None, None, :], block, 0.0)
    from_x = exchange(carried, 1)
    from_y = exchange(carried, 2)
    blocks = [block]
    for k in range(1, win_count):
        blocks.append(along_win(block, k))

    def first_body(*refs):
        scal, owner = position(), refs[0]
        tables = refs[1 : 1 + win_count]
        diag, x_out, prm, s_emb, x_ref, work, s_planes = refs[1 + win_count :]
        z_re, z_im, weight_re, weight_im = contour(scal, owner, tables, dims, point_count)
        for k, value in enumerate((z_re, z_im, weight_re, weight_im)):
            prm[k] = value
        eye = eye_of(n)
        x_out[...] = packed_pair(
            invert(z_re * eye - diag[0, 0], z_im * eye - diag[0, 1], z_im, s_emb, x_ref, work, s_planes)
        )

    head = [owner_order] + tables
    head_specs = [smem] * len(head)
    first = pl.pallas_call(
        first_body,
        out_shape=[pair_shape, jax.ShapeDtypeStruct((4,), F32)],
        in_specs=head_specs + [vmem],
        out_specs=[vmem, smem],
        scratch_shapes=scratch,
        cost_estimate=lasting(6),
        compiler_params=grant,
    )
    x_own, prm = first(*head, diag_blocks)

    relay = jnp.where(lax.axis_index("point") == 0, from_y, from_x)
    flat = [(2 * s, 2 * (s ^ 1)) for s in range(slab_count)]
    flat += [(2 * s + 1, 2 * (s ^ 2) + 1) for s in range(slab_count)]
    from_far = lax.ppermute(relay, ("slab", "point"), flat)
    from_x = (from_x, swap(from_x))
    from_y = (from_y, swap(from_y))
    from_far = (from_far, swap(from_far))

    def second_body(*refs):
        scal, prm = position(), refs[0]
        (x_own, own_c, x_dir, x_swp, x_out, w_out, l_out, s_emb, x_ref, work, s_planes) = refs[1:]
        z_re, z_im = prm[0], prm[1]
        p = scal[2]
        near = [rows_of(x_dir, x_swp, k, p) for k in range(3)]
        even = lax.rem(scal[1], 2) == 0
        re, im, adj_re, adj_im = oriented(even, (own_c[0, 0], own_c[0, 1]), (near[1], near[2]))
        solved = product(x_own[...], jnp.concatenate([re, im], 1))
        w_out[...] = packed_pair(solved)
        left = packed_pair(jnp.concatenate([adj_re, adj_im], 1))
        l_out[...] = left
        update = product(left, solved)
        d_re, d_im = unpack_diag(near[0])
        eye = eye_of(n)
        x_out[...] = packed_pair(
            invert(
                z_re * eye - d_re - update[:, :n],
                z_im * eye - d_im - update[:, n:],
                z_im,
                s_emb,
                x_ref,
                work,
                s_planes,
            )
        )

    second = pl.pallas_call(
        second_body,
        out_shape=[pair_shape] * 3,
        in_specs=[smem] + [vmem] * 4,
        out_specs=[vmem] * 3,
        scratch_shapes=scratch,
        cost_estimate=lasting(8),
        compiler_params=grant,
    )
    x_near, w_near, l_near = second(prm, x_own, couplings, *from_x)

    def third_body(*refs):
        scal, prm = position(), refs[0]
        (x_own, x_near, l_near, own_c, x_dir, x_swp, y_dir, y_swp) = refs[1:9]
        (x_out, w_out, l_out, ahead, later, s_emb, x_ref, work, s_planes, s_ref) = refs[9:]
        for k in range(4):
            later[k] = prm[k]
        z_re, z_im = prm[0], prm[1]
        p = scal[2]
        even = lax.rem(scal[1], 2) == 0
        chain = lax.rem(scal[1], 2) == scal[1] // 2
        odd_fork = jnp.logical_not(jnp.logical_or(chain, even))
        even_fork = jnp.logical_and(jnp.logical_not(chain), even)
        d_re, d_im = unpack_diag(rows_of(y_dir, y_swp, 0, p))
        eye = eye_of(n)
        s_ref[...] = jnp.concatenate([z_re * eye - d_re, z_im * eye - d_im], 1)

        @pl.when(chain)
        def _():
            re, im, adj_re, adj_im = oriented(
                even,
                [rows_of(x_dir, x_swp, k, p) for k in (1, 2)],
                [rows_of(y_dir, y_swp, k, p) for k in (1, 2)],
            )
            solved = product(x_near[...], jnp.concatenate([re, im], 1))
            w_out[...] = packed_pair(solved)
            left = packed_pair(jnp.concatenate([adj_re, adj_im], 1))
            l_out[...] = left
            s_ref[...] = s_ref[...] - product(left, solved)

        @pl.when(odd_fork)
        def _():
            cross = product(x_own[...], jnp.concatenate([own_c[0, 0], own_c[0, 1]], 1))
            w_out[...] = packed_pair(cross)
            l_out[...] = packed_pair(jnp.concatenate([own_c[0, 0].T, -own_c[0, 1].T], 1))
            ahead[...] = product(l_near[...], cross)

        x_pair = packed_pair(invert(s_ref[:, :n], s_ref[:, n:], z_im, s_emb, x_ref, work, s_planes))
        x_out[...] = x_pair

        @pl.when(even_fork)
        def _():
            re, im = [rows_of(y_dir, y_swp, k, p) for k in (1, 2)]
            solved = product(x_pair, jnp.concatenate([re, im], 1))
            w_out[...] = packed_pair(solved)
            left = packed_pair(jnp.concatenate([re.T, -im.T], 1))
            l_out[...] = left
            ahead[...] = product(left, solved)

    wide_shape = jax.ShapeDtypeStruct((n, 2 * n), F32)
    x_side, w_mid, l_mid, ahead, later = pl.pallas_call(
        third_body,
        out_shape=[pair_shape] * 3 + [wide_shape, jax.ShapeDtypeStruct((4,), F32)],
        in_specs=[smem] + [vmem] * 8,
        out_specs=[vmem] * 4 + [smem],
        scratch_shapes=scratch + [pltpu.VMEM((n, 2 * n), F32)],
        cost_estimate=lasting(8),
        compiler_params=grant,
    )(prm, x_own, x_near, l_near, couplings, *from_x, *from_y)

    def route_body(*refs):
        scal, owner = position(), refs[0]
        blocks = refs[1 : 1 + win_count]
        out = refs[2 + win_count]
        lane = lax.broadcasted_iota(jnp.int32, (half, lanes), 1)
        for k in range(slab_count):
            target = scal[1] ^ k
            part = lax.rem(target, parts)
            shift, index = slot_of(scal, owner, target, dims)
            for k_win in range(win_count):

                @pl.when(shift == k_win)
                def _():
                    re = blocks[k_win][index, 0]
                    im = blocks[k_win][index, 1]
                    mine = jnp.where(
                        part == 0,
                        jnp.where(lane < width, re, pltpu.roll(im, width, 1)),
                        jnp.where(lane < width, pltpu.roll(re, width, 1), im),
                    )
                    out[k] = mine

    piece = jax.ShapeDtypeStruct((half, lanes), F32)
    quad = jax.ShapeDtypeStruct((slab_count, half, lanes), F32)
    routed = pl.pallas_call(
        route_body,
        out_shape=quad,
        in_specs=[smem] + [vmem] * win_count + [smem],
        out_specs=vmem,
        cost_estimate=lasting(2),
        compiler_params=grant,
    )(owner_order, *blocks, later)

    def join_body(mine, other, *outs):
        p = position()[2]
        for k in range(slab_count):
            outs[k][pl.ds(p * half, half), :] = mine[k]
            outs[k][pl.ds((1 - p) * half, half), :] = other[k]

    joined = pl.pallas_call(
        join_body,
        out_shape=[jax.ShapeDtypeStruct((n, lanes), F32)] * slab_count,
        in_specs=[vmem] * 2,
        out_specs=[vmem] * slab_count,
        compiler_params=grant,
    )(routed, swap(routed))
    rhs = [joined[0]] + [exchange(joined[k], k) for k in range(1, slab_count)]

    def fourth_body(*refs):
        scal, prm = position(), refs[0]
        (x_own, x_near, x_side, w_near, l_near, w_mid, l_mid, ahead, y_dir, y_swp, f_dir, f_swp) = refs[1:13]
        (x_out, w_far, l_far, w_cross, l_cross, w_last, l_last, s_emb, x_ref, work, s_planes, s_ref, fill) = refs[13:]
        z_re, z_im = prm[0], prm[1]
        p = scal[2]
        even = lax.rem(scal[1], 2) == 0
        chain = lax.rem(scal[1], 2) == scal[1] // 2
        far = [rows_of(f_dir, f_swp, k, p) for k in range(3)]
        side = [rows_of(y_dir, y_swp, k, p) for k in (1, 2)]
        d_re, d_im = unpack_diag(far[0])
        eye = eye_of(n)
        s_ref[...] = jnp.concatenate([z_re * eye - d_re, z_im * eye - d_im], 1)

        @pl.when(chain)
        def _():
            zero = jnp.zeros((n, 4 * n), BF16)
            w_cross[...] = zero
            l_cross[...] = zero
            w_far[...] = w_mid[...]
            l_far[...] = l_mid[...]

        odd_fork = jnp.logical_not(jnp.logical_or(chain, even))
        even_fork = jnp.logical_and(jnp.logical_not(chain), even)

        @pl.when(odd_fork)
        def _():
            w_cross[...] = w_mid[...]
            l_cross[...] = l_mid[...]
            fill[...] = ahead[...]

        @pl.when(even_fork)
        def _():
            cross = product(x_own[...], jnp.concatenate([far[1].T, -far[2].T], 1))
            w_cross[...] = packed_pair(cross)
            l_cross[...] = packed_pair(jnp.concatenate([far[1], far[2]], 1))
            fill[...] = product(l_near[...], cross)

        @pl.when(jnp.logical_not(chain))
        def _():
            back = packed_pair(product(l_cross[...], whole(w_near[...])))
            l_far[...] = back
            solved = product(x_near[...], fill[...])
            w_far[...] = packed_pair(solved)
            s_ref[...] = (
                s_ref[...] - product(l_cross[...], whole(w_cross[...])) - product(back, solved)
            )

        @pl.when(even_fork)
        def _():
            w_last[...] = w_mid[...]
            l_last[...] = l_mid[...]
            s_ref[...] = s_ref[...] - ahead[...]

        @pl.when(jnp.logical_not(even_fork))
        def _():
            re, im, adj_re, adj_im = oriented(even, side, (far[1], far[2]))
            solved = product(x_side[...], jnp.concatenate([re, im], 1))
            w_last[...] = packed_pair(solved)
            left = packed_pair(jnp.concatenate([adj_re, adj_im], 1))
            l_last[...] = left
            s_ref[...] = s_ref[...] - product(left, solved)

        s_now = s_ref[...]
        x_out[...] = packed_pair(invert(s_now[:, :n], s_now[:, n:], z_im, s_emb, x_ref, work, s_planes))

    x_far, w_far, l_far, w_cross, l_cross, w_last, l_last = pl.pallas_call(
        fourth_body,
        out_shape=[pair_shape] * 7,
        in_specs=[smem] + [vmem] * 12,
        out_specs=[vmem] * 7,
        scratch_shapes=scratch + [pltpu.VMEM((n, 2 * n), F32)] * 2,
        cost_estimate=lasting(10),
        compiler_params=grant,
    )(prm, x_own, x_near, x_side, w_near, l_near, w_mid, l_mid, ahead, *from_y, *from_far)

    def solve_body(*refs):
        scal, prm = position(), refs[0]
        (x_own, x_near, x_side, x_far, w_near, l_near, w_cross, l_cross, w_far, l_far, w_last, l_last) = refs[1:13]
        loaded = refs[13:17]
        keep, send = refs[17:]
        weight_re, weight_im = prm[2], prm[3]
        p = scal[2]
        chain = lax.rem(scal[1], 2) == scal[1] // 2

        def apply(ref, value):
            pair = ref[...]
            high, low = hi_lo(jnp.concatenate([value, times_i(value)], 0))
            wide = dot(pair[:, : 2 * n], jnp.concatenate([high, low], 1))
            return wide[:, :lanes] + wide[:, lanes:] + dot(pair[:, 2 * n :], high)

        b_own, b_near, b_side, b_far = [ref[...] for ref in loaded]
        u_own = apply(x_own, b_own)
        b_near = b_near + apply(l_near, u_own)
        b_far = b_far + apply(l_cross, u_own)
        u_near = apply(x_near, b_near)
        step = apply(l_far, u_near)
        b_side = b_side + pick(chain, step, 0.0)
        b_far = b_far + pick(chain, 0.0, step)
        u_side = apply(x_side, b_side)
        b_far = b_far + apply(l_last, u_side)
        far = apply(x_far, b_far)
        side = u_side + apply(w_last, far)
        near = u_near + apply(w_far, pick(chain, side, far))
        own = u_own + apply(w_near, near) + apply(w_cross, far)
        for k, value in enumerate((own, near, side, far)):
            value = weight_re * value + weight_im * times_i(value)
            keep[k] = pick(p == 0, value[:half], value[half:])
            send[k] = pick(p == 0, value[half:], value[:half])

    keep, send = pl.pallas_call(
        solve_body,
        out_shape=[quad] * 2,
        in_specs=[smem] + [vmem] * 16,
        out_specs=[vmem] * 2,
        cost_estimate=lasting(8),
        compiler_params=grant,
    )(
        prm, x_own, x_near, x_side, x_far, w_near, l_near, w_cross, l_cross, w_far, l_far, w_last, l_last, *rhs
    )

    def add_body(keep, send, *outs):
        for k in range(slab_count):
            outs[k][...] = keep[k] + send[k]

    total = pl.pallas_call(
        add_body,
        out_shape=[piece] * slab_count,
        in_specs=[vmem] * 2,
        out_specs=[vmem] * slab_count,
        compiler_params=grant,
    )(keep, swap(send))
    shares = [total[0]] + [exchange(total[k], k) for k in range(1, slab_count)]

    def place_body(*refs):
        scal = position()
        shares = refs[:slab_count]
        out = refs[slab_count]
        lane = lax.broadcasted_iota(jnp.int32, (half, lanes), 1)
        for slot in range(local_count):
            found = []
            for part in range(parts):
                distance = scal[1] ^ (slot * parts + part)
                value = shares[0][...]
                for k in range(1, slab_count):
                    value = jnp.where(distance == k, shares[k][...], value)
                found.append(value)
            low, high = found
            out[slot, 0, 0] = jnp.where(lane < width, low, pltpu.roll(high, width, 1))
            out[slot, 0, 1] = jnp.where(lane < width, pltpu.roll(low, width, 1), high)

    return pl.pallas_call(
        place_body,
        out_shape=jax.ShapeDtypeStruct((local_count, 1, 2, half, columns), F32),
        in_specs=[vmem] * slab_count,
        out_specs=vmem,
        compiler_params=grant,
    )(*shares)


def solution(mesh):
    placed = (
        P("slab", None, None, None),
        P("slab", None, None, None),
        P("win", "slab", None, None, None),
        P("win"),
        P(),
        P("win"),
        P("win"),
    )

    return jax.shard_map(
        per_device,
        mesh=mesh,
        in_specs=placed,
        out_specs=P("win", "slab", None, "point", None),
        check_vma=False,
    )
```
